32 devices in a mesh: section: 4 (over z), seq: 8 (over y, x, core).
Axes of the slice: x: 2, y: 2, z: 4, core: 2. Of those that a mesh axis runs over, the one named last changes fastest.
Arguments:
- queries: bfloat16 [4, 2, 1024, 4096], P('section', None, 'seq'), may hold values from -80 to 80
- keys_new: bfloat16 [4, 2, 1024, 1024], P('section', None, 'seq'), may hold values from -4 to 4
- values_new: bfloat16 [4, 2, 1024, 1024], P('section', None, 'seq'), may hold values from -6 to 6
- key_cache: bfloat16 [4, 32, 4096, 128], P('section', 'seq'), may hold values from -6 to 6
- value_cache: bfloat16 [4, 32, 4096, 128], P('section', 'seq'), may hold values from -6 to 6
- block_lists: int32 [4, 32, 2, 16, 32], P('section', 'seq'), may hold values from 0 to 63, as said below
- block_counts: int32 [4, 32, 2, 16], P('section', 'seq'), may hold values from 1 to 32
- visible_blocks: int32 [2], replicated, may hold values from 32 to 64
Outputs:
- handed: bfloat16 [4, 2, 1024, 4096], P('section', None, 'seq')
The draws below stay inside these ranges and needn't reach their ends.
Inputs may be any that keep to these rules, and one draw needn't show every extreme that they name: `block_lists`: each list holds 32 different block numbers.
All inputs are finite; a program needn't handle non-finite values.
Results may differ from the reference program's by a relative error of at most 0.003.
Values may be sent and summed in bfloat16 or wider, within the bound.
A program may use at most 192 MiB of HBM per device.

```python
from functools import partial
import jax
import jax.numpy as jnp
from jax import lax

HEADS = 32
KVH = 8
DH = 128
SPAN = 1024
SPANS = 2
BLK = 64
CTX = 4096
NSEL = 32
LAYERS = 4
QBLOCKS = 16
CACHE_BLOCKS = 64


def joint_draw(key):
    key_query, key_keys = jax.random.split(jax.random.fold_in(key, 7))
    group_size = HEADS // KVH
    keys_drawn = jnp.clip(jax.random.normal(key_keys, (LAYERS, SPANS, SPAN, KVH, 1, DH), jnp.float32), -4.0, 4.0)
    query_drawn = jnp.clip(2.5 * jax.random.normal(key_query, (LAYERS, SPANS, SPAN, KVH, group_size, DH), jnp.float32), -12.0, 12.0)
    query_out = query_drawn.reshape(LAYERS, SPANS, SPAN, HEADS * DH)
    keys_out = keys_drawn.reshape(LAYERS, SPANS, SPAN, KVH * DH)
    return (query_out, keys_out)


def draw_queries(key, part):
    return joint_draw(key)[0].astype(jnp.bfloat16)


def draw_keys_new(key, part):
    return joint_draw(key)[1].astype(jnp.bfloat16)


def pick_permutation(sub_key):
    return jax.random.permutation(sub_key, CACHE_BLOCKS)


def draw_block_lists(key, part):
    list_total = LAYERS * HEADS * SPANS * QBLOCKS
    sub_keys = jax.random.split(jax.random.fold_in(key, 21), list_total)
    chosen = jax.vmap(pick_permutation)(sub_keys)[:, :NSEL]
    return chosen.reshape(LAYERS, HEADS, SPANS, QBLOCKS, NSEL).astype(jnp.int32)


def draw_block_counts(key, part):
    key_cap, key_raw, key_spot = jax.random.split(jax.random.fold_in(key, 33), 3)
    head_cap = jax.random.randint(key_cap, (LAYERS, HEADS, 1, 1), NSEL // 4, NSEL + 1)
    raw_value = jax.random.randint(key_raw, (LAYERS, HEADS, SPANS, QBLOCKS), 0, 1 << 20)
    counted = 1 + raw_value % head_cap
    list_total = LAYERS * HEADS * SPANS * QBLOCKS
    spot_index = jax.random.randint(key_spot, (), 0, list_total)
    flat_counts = jnp.where(jnp.arange(list_total) == spot_index, NSEL, counted.reshape(list_total))
    return flat_counts.reshape(LAYERS, HEADS, SPANS, QBLOCKS).astype(jnp.int32)


def levels(rng, extent, shards, smallest, top_value):
    gain, own = 1.0, jax.random.fold_in(rng, 6)
    for dim, blocks in shards:
        heights = jnp.exp(jax.random.uniform(jax.random.fold_in(own, dim), (blocks,), jnp.float32, smallest / len(shards), top_value / len(shards)))
        gain = gain * jnp.repeat(heights, extent[dim] // blocks).reshape([-1 if axis == dim else 1 for axis in range(len(extent))])
    return gain


def bell_draw(stream_key, dims, width, limit, cuts=(), kind=jnp.bfloat16):
    gain = levels(stream_key, dims, cuts, -0.22, 0.18) if cuts else 1.0
    result = jax.random.normal(stream_key, dims, jnp.float32) * width * gain
    return jnp.minimum(jnp.maximum(result, -limit), limit).astype(kind)


def setup_inputs(seed: int = 0) -> dict:
    splits = jax.random.split(jax.random.key(seed), 9)
    return {
        "queries": draw_queries(jax.random.fold_in(splits[8], 71), 0),
        "keys_new": draw_keys_new(jax.random.fold_in(splits[8], 71), 0),
        "values_new": bell_draw(splits[2], (LAYERS, SPANS, SPAN, KVH * DH), 1.0, 6.0, ((0, 4), (2, 8))),
        "key_cache": bell_draw(splits[3], (LAYERS, HEADS, CTX, DH), 1.0, 6.0, ((0, 4), (1, 8))),
        "value_cache": bell_draw(splits[4], (LAYERS, HEADS, CTX, DH), 1.0, 6.0, ((0, 4), (1, 8))),
        "block_lists": draw_block_lists(jax.random.fold_in(splits[8], 71), 0),
        "block_counts": draw_block_counts(jax.random.fold_in(splits[8], 71), 0),
        "visible_blocks": jax.random.randint(splits[7], (SPANS,), CACHE_BLOCKS // 2, CACHE_BLOCKS + 1).astype(jnp.int32),
    }


def head_attention(visible_blocks, items):
    query_head, key_head, value_head, cache_keys, cache_values, lists_head, counts_head = items
    score_scale = 1.0 / (DH ** 0.5)
    results = []
    for span_index in range(SPANS):
        query_float = query_head[span_index].astype(jnp.float32)
        own_scores = jnp.einsum("rd,kd->rk", query_float, key_head[span_index].astype(jnp.float32), precision=lax.Precision.HIGHEST) * score_scale
        causal = jnp.arange(SPAN)[:, None] >= jnp.arange(SPAN)[None, :]
        own_scores = jnp.where(causal, own_scores, -jnp.inf)
        chosen = lists_head[span_index]
        key_blocks = cache_keys[chosen].astype(jnp.float32)
        cache_scores = jnp.einsum("qbd,qjtd->qbjt", query_float.reshape(QBLOCKS, BLK, DH), key_blocks, precision=lax.Precision.HIGHEST) * score_scale
        usable = (jnp.arange(NSEL)[None, :] < counts_head[span_index][:, None]) & (chosen < visible_blocks[span_index])
        cache_scores = jnp.where(usable[:, None, :, None], cache_scores, -jnp.inf).reshape(QBLOCKS, BLK, NSEL * BLK)
        every_score = jnp.concatenate([cache_scores, own_scores.reshape(QBLOCKS, BLK, SPAN)], axis=2)
        row_max = jnp.max(every_score, axis=2, keepdims=True)
        weights = jnp.exp(every_score - row_max)
        row_sum = jnp.sum(weights, axis=2)
        weights_b = weights.astype(jnp.bfloat16).astype(jnp.float32)
        value_blocks = cache_values[chosen].astype(jnp.float32).reshape(QBLOCKS, NSEL * BLK, DH)
        mixed = jnp.einsum("qbk,qkd->qbd", weights_b[:, :, :NSEL * BLK], value_blocks, precision=lax.Precision.HIGHEST)
        mixed = mixed + jnp.einsum("qbk,kd->qbd", weights_b[:, :, NSEL * BLK:], value_head[span_index].astype(jnp.float32), precision=lax.Precision.HIGHEST)
        results.append((mixed / row_sum[:, :, None]).astype(jnp.bfloat16).reshape(SPAN, DH))
    return jnp.stack(results)


def reference(queries, keys_new, values_new, key_cache, value_cache, block_lists, block_counts, visible_blocks):
    group_size = HEADS // KVH
    layers = queries.shape[0]
    query_heads = queries.reshape(layers, SPANS, SPAN, HEADS, DH).transpose(0, 3, 1, 2, 4).reshape(layers * HEADS, SPANS, SPAN, DH)
    key_heads = jnp.repeat(keys_new.reshape(layers, SPANS, SPAN, KVH, DH), group_size, axis=3)
    key_heads = key_heads.transpose(0, 3, 1, 2, 4).reshape(layers * HEADS, SPANS, SPAN, DH)
    value_heads = jnp.repeat(values_new.reshape(layers, SPANS, SPAN, KVH, DH), group_size, axis=3)
    value_heads = value_heads.transpose(0, 3, 1, 2, 4).reshape(layers * HEADS, SPANS, SPAN, DH)
    cache_keys = key_cache.reshape(layers * HEADS, CACHE_BLOCKS, BLK, DH)
    cache_values = value_cache.reshape(layers * HEADS, CACHE_BLOCKS, BLK, DH)
    lists_all = block_lists.reshape(layers * HEADS, SPANS, QBLOCKS, NSEL)
    counts_all = block_counts.reshape(layers * HEADS, SPANS, QBLOCKS)
    outputs = lax.map(partial(head_attention, visible_blocks), (query_heads, key_heads, value_heads, cache_keys, cache_values, lists_all, counts_all))
    attended = outputs.reshape(layers, HEADS, SPANS, SPAN, DH).transpose(0, 2, 3, 1, 4).reshape(layers, SPANS, SPAN, HEADS * DH)
    return jnp.roll(attended, 1, axis=0)
```

```python
import functools
import math

import jax
import jax.numpy as jnp
from jax import lax
from jax.experimental import pallas as pl
from jax.experimental.pallas import tpu as pltpu
from jax.sharding import PartitionSpec as P

DH = 128
BLK = 64
GROUP = 4
LANES = 128
ROW_TILE = 256
CHUNK = 512
FAR = -1e30


def mesh_copy(src, dst, send_sem, recv_sem, section, seq):
    return pltpu.make_async_remote_copy(
        src_ref=src,
        dst_ref=dst,
        send_sem=send_sem,
        recv_sem=recv_sem,
        device_id=(section, seq),
        device_id_type=pl.DeviceIdType.MESH,
    )


def scores_of(query, keys):
    return lax.dot_general(
        query, keys, (((1,), (1,)), ((), ())), preferred_element_type=jnp.float32
    )


def whole_max(best, scores):
    for i in range(0, scores.shape[1], LANES):
        part = scores[:, i : i + LANES]
        best = part if best is None else jnp.maximum(best, part)
    return best


def fused(
    n,
    sections,
    visible,
    lists,
    counts,
    queries,
    keys_new,
    values_new,
    key_cache,
    value_cache,
    out,
    qbuf,
    kbuf,
    vbuf,
    ckeys,
    cvalues,
    reach,
    att,
    score_buf,
    top_buf,
    in_send,
    in_recv,
    in_local,
    cache_sem,
    out_send,
    out_recv,
):
    spans, heads, span_len = qbuf.shape[0], qbuf.shape[1], qbuf.shape[2]
    context = ckeys.shape[1]
    kv_dev = kbuf.shape[1]
    rows = queries.shape[2]
    slots = lists.shape[1]
    query_blocks = span_len // BLK
    items = 2 * kv_dev + heads
    tiles = span_len // ROW_TILE
    columns = reach.shape[1]
    weight_scale = math.log2(math.e) / math.sqrt(DH)
    section = lax.axis_index("section")
    me = lax.axis_index("seq")
    above = lax.rem(section + 1, sections)
    below = lax.rem(section + sections - 1, sections)

    def key_copy(head):
        return pltpu.make_async_copy(key_cache.at[0, head], ckeys.at[head], cache_sem.at[0, head])

    def value_copy(head):
        return pltpu.make_async_copy(
            value_cache.at[0, head], cvalues.at[head], cache_sem.at[1, head]
        )

    def source(span, item, seq):
        if isinstance(item, int) and item < 2 * kv_dev:
            array = keys_new if item < kv_dev else values_new
            column = lax.div(seq * heads, GROUP) * DH + (item % kv_dev) * DH
        else:
            array = queries
            column = (seq * heads + item - 2 * kv_dev) * DH
        return array.at[0, span, :, pl.ds(pl.multiple_of(column, DH), DH)]

    def landing(span, item, seq):
        where = pl.ds(pl.multiple_of(seq * rows, rows), rows)
        if isinstance(item, int) and item < kv_dev:
            return kbuf.at[span, item, where, :]
        if isinstance(item, int) and item < 2 * kv_dev:
            return vbuf.at[span, item - kv_dev, where, :]
        return qbuf.at[span, item - 2 * kv_dev, where, :]

    def own_copy(span, item):
        return pltpu.make_async_copy(
            source(span, item, me), landing(span, item, me), in_local.at[span, item]
        )

    for span in range(spans):
        for item in range(items):
            own_copy(span, item).start()

    barrier = pltpu.get_barrier_semaphore()

    def greet(k, carry):
        @pl.when(k > 0)
        def _():
            pl.semaphore_signal(
                barrier,
                inc=1,
                device_id=(section, lax.rem(me + k, n)),
                device_id_type=pl.DeviceIdType.MESH,
            )

        for there in (above, below):
            pl.semaphore_signal(
                barrier,
                inc=1,
                device_id=(there, lax.rem(me + k, n)),
                device_id_type=pl.DeviceIdType.MESH,
            )
        return carry

    lax.fori_loop(0, n, greet, 0)
    pl.semaphore_wait(barrier, 3 * n - 1)

    for head in range(heads):
        key_copy(head).start()
        value_copy(head).start()

    def in_copy(span, item, k, seq_to, seq_from):
        return mesh_copy(
            source(span, item, seq_to),
            landing(span, item, seq_from),
            in_send.at[span, item, k],
            in_recv.at[span, item, k],
            section,
            seq_to,
        )

    for span in range(spans):
        for item in range(items):

            def send_in(k, carry):
                in_copy(span, item, k, lax.rem(me + k, n), me).start()
                return carry

            lax.fori_loop(1, n, send_in, 0)

    def await_in(span, item):
        own_copy(span, item).wait()

        def one(k, carry):
            in_copy(
                span, item, k, lax.rem(me + k, n), lax.rem(me + n - k, n)
            ).wait_recv()
            return carry

        lax.fori_loop(1, n, one, 0)

    def out_copy(span, head, k, seq_to, seq_from):
        column = pl.multiple_of((seq_from * heads + head) * DH, DH)
        return mesh_copy(
            att.at[span, head, pl.ds(pl.multiple_of(seq_to * rows, rows), rows), :],
            out.at[0, span, :, pl.ds(column, DH)],
            out_send.at[span, head, k],
            out_recv.at[span, head, k],
            above,
            seq_to,
        )

    def build_reach():
        lane = lax.broadcasted_iota(jnp.int32, (1, columns), 1)
        group = lax.div(lane, query_blocks)
        count = jnp.zeros((1, columns), jnp.float32)
        place = lax.rem(lax.broadcasted_iota(jnp.int32, (query_blocks, columns), 1), query_blocks)
        spread = jnp.where(
            place == lax.broadcasted_iota(jnp.int32, (query_blocks, columns), 0), 1.0, 0.0
        ).astype(jnp.bfloat16)
        span_at = lax.broadcasted_iota(jnp.int32, (spans, columns), 0)
        group_at = lax.div(lax.broadcasted_iota(jnp.int32, (spans, columns), 1), query_blocks)
        for head in range(heads):
            wide = jnp.dot(
                counts[0, head].astype(jnp.float32).astype(jnp.bfloat16),
                spread,
                preferred_element_type=jnp.float32,
            )
            wide = jnp.where(group_at == head * spans + span_at, wide, 0.0)
            count = count + jnp.sum(wide, axis=0, keepdims=True)
        seen = jnp.zeros((1, columns), jnp.int32)
        for span in range(spans):
            seen = jnp.where(lax.rem(group, spans) == span, visible[span], seen)
        seen = seen.astype(jnp.float32)
        eye = jnp.where(
            lax.broadcasted_iota(jnp.int32, (slots, slots), 0)
            == lax.broadcasted_iota(jnp.int32, (slots, slots), 1),
            1.0,
            0.0,
        ).astype(jnp.bfloat16)
        listed = lists[...].astype(jnp.float32)
        if columns > listed.shape[0]:
            listed = jnp.concatenate(
                [listed, jnp.zeros((columns - listed.shape[0], slots), jnp.float32)], axis=0
            )
        listed = scores_of(eye, listed.astype(jnp.bfloat16))
        slot = lax.broadcasted_iota(jnp.int32, (slots, columns), 0).astype(jnp.float32)
        listed = jnp.where((slot < count) & (listed < seen), listed, -1.0)
        blocks = context // BLK
        block = lax.broadcasted_iota(jnp.int32, (blocks, columns), 0).astype(jnp.float32)
        bias = jnp.full((blocks, columns), FAR, jnp.float32)
        for i in range(slots):
            bias = jnp.where(listed[i : i + 1, :] == block, 0.0, bias)
        for j in range(blocks):
            reach[j * BLK : (j + 1) * BLK, :] = jnp.broadcast_to(
                bias[j : j + 1, :], (BLK, columns)
            ).astype(jnp.bfloat16)

    build_reach()

    row_at = lax.broadcasted_iota(jnp.int32, (ROW_TILE, ROW_TILE), 0)
    key_at = lax.broadcasted_iota(jnp.int32, (ROW_TILE, ROW_TILE), 1)
    mark_row = lax.div(lax.broadcasted_iota(jnp.int32, (ROW_TILE, columns), 0), BLK)
    mark_lane = lax.broadcasted_iota(jnp.int32, (ROW_TILE, columns), 1)

    def score_steps(span, head, kv, tile):
        slot = tile % 2
        at = slice(tile * ROW_TILE, (tile + 1) * ROW_TILE)
        best = [None]
        first = (head * spans + span) * query_blocks + tile * (ROW_TILE // BLK)

        def keep(scores, start):
            score_buf[slot, :, start : start + scores.shape[1]] = scores
            best[0] = whole_max(best[0], scores)

        def cache(start):
            mark = jnp.where(mark_lane == mark_row + first, 1.0, 0.0).astype(jnp.bfloat16)
            query = jnp.concatenate([qbuf[span, head, at, :], mark], axis=1)
            keys = jnp.concatenate(
                [ckeys[head, start : start + CHUNK, :], reach[start : start + CHUNK, :]], axis=1
            )
            keep(scores_of(query, keys), start)

        def own(piece):
            keys = kbuf[span, kv, piece * ROW_TILE : (piece + 1) * ROW_TILE, :]
            scores = scores_of(qbuf[span, head, at, :], keys)
            if piece == tile:
                scores = jnp.where(row_at >= key_at, scores, FAR)
            keep(scores, context + piece * ROW_TILE)

        def finish():
            top = jnp.max(best[0], axis=1, keepdims=True)
            top_buf[slot] = jnp.broadcast_to(top, (ROW_TILE, LANES))

        return (
            [functools.partial(cache, start) for start in range(0, context, CHUNK)]
            + [functools.partial(own, piece) for piece in range(tile + 1)]
            + [finish]
        )

    def value_steps(span, head, kv, tile):
        slot = tile % 2
        total = [None]

        def part(start, values):
            top = top_buf[slot]
            size = values.shape[0]
            weights = []
            for i in range(start, start + size, LANES):
                scores = score_buf[slot, :, i : i + LANES]
                weights.append(jnp.exp2((scores - top) * weight_scale).astype(jnp.bfloat16))
            values = jnp.concatenate([values, jnp.ones((size, LANES), jnp.bfloat16)], axis=1)
            product = jnp.dot(
                jnp.concatenate(weights, axis=1), values, preferred_element_type=jnp.float32
            )
            total[0] = product if total[0] is None else total[0] + product

        def cache(start):
            part(start, cvalues[head, start : start + CHUNK, :])

        def own(piece):
            part(
                context + piece * ROW_TILE,
                vbuf[span, kv, piece * ROW_TILE : (piece + 1) * ROW_TILE, :],
            )

        def finish():
            mixed = total[0][:, :DH] / total[0][:, DH:]
            att[span, head, tile * ROW_TILE : (tile + 1) * ROW_TILE, :] = mixed.astype(
                jnp.bfloat16
            )

        return (
            [functools.partial(cache, start) for start in range(0, context, CHUNK)]
            + [functools.partial(own, piece) for piece in range(tile + 1)]
            + [finish]
        )

    def one_unit(unit, carry):
        span, head = lax.div(unit, heads), lax.rem(unit, heads)
        kv = lax.div(head, GROUP)

        @pl.when(head == 0)
        def _():
            for item in range(2 * kv_dev):
                await_in(span, item)

        @pl.when(span == 0)
        def _():
            key_copy(head).wait()
            value_copy(head).wait()

        await_in(span, 2 * kv_dev + head)
        for step in score_steps(span, head, kv, 0):
            step()
        for tile in range(tiles):
            now = value_steps(span, head, kv, tile)
            later = score_steps(span, head, kv, tile + 1) if tile + 1 < tiles else []
            for i in range(max(len(now), len(later))):
                if i < len(later):
                    later[i]()
                if i < len(now):
                    now[i]()

        def send_out(k, inner):
            out_copy(span, head, k, lax.rem(me + k, n), me).start()
            return inner

        lax.fori_loop(0, n, send_out, 0)
        return carry

    lax.fori_loop(0, spans * heads, one_unit, 0)

    for span in range(spans):
        for item in range(items):

            def sent(k, carry):
                in_copy(span, item, k, lax.rem(me + k, n), me).wait_send()
                return carry

            lax.fori_loop(1, n, sent, 0)

        def head_done(head, carry):
            def both(k, inner):
                out_copy(span, head, k, lax.rem(me + k, n), me).wait_send()
                out_copy(
                    span, head, k, lax.rem(me + k, n), lax.rem(me + n - k, n)
                ).wait_recv()
                return inner

            return lax.fori_loop(0, n, both, carry)

        lax.fori_loop(0, heads, head_done, 0)


def on_device(
    queries, keys_new, values_new, key_cache, value_cache, block_lists, block_counts, visible_blocks
):
    n = lax.axis_size("seq")
    sections = lax.axis_size("section")
    spans, rows = queries.shape[1], queries.shape[2]
    heads, context = key_cache.shape[1], key_cache.shape[2]
    kv_dev = max(1, heads // GROUP)
    span_len = rows * n
    items = 2 * kv_dev + heads
    slots = block_lists.shape[4]
    smem = pl.BlockSpec(memory_space=pltpu.MemorySpace.SMEM)
    vmem = pl.BlockSpec(memory_space=pltpu.MemorySpace.VMEM)
    anywhere = pl.BlockSpec(memory_space=pl.ANY)
    cols = -(-heads * spans * (span_len // BLK) // LANES) * LANES
    dma = pltpu.SemaphoreType.DMA
    return pl.pallas_call(
        functools.partial(fused, n, sections),
        out_shape=jax.ShapeDtypeStruct(queries.shape, queries.dtype),
        in_specs=[smem, vmem, vmem] + [anywhere] * 5,
        out_specs=anywhere,
        scratch_shapes=[
            pltpu.VMEM((spans, heads, span_len, DH), jnp.bfloat16),
            pltpu.VMEM((spans, kv_dev, span_len, DH), jnp.bfloat16),
            pltpu.VMEM((spans, kv_dev, span_len, DH), jnp.bfloat16),
            pltpu.VMEM((heads, context, DH), jnp.bfloat16),
            pltpu.VMEM((heads, context, DH), jnp.bfloat16),
            pltpu.VMEM((context, cols), jnp.bfloat16),
            pltpu.VMEM((spans, heads, span_len, DH), jnp.bfloat16),
            pltpu.VMEM((2, ROW_TILE, context + span_len), jnp.float32),
            pltpu.VMEM((2, ROW_TILE, LANES), jnp.float32),
            dma((spans, items, n)),
            dma((spans, items, n)),
            dma((spans, items)),
            dma((2, heads)),
            dma((spans, heads, n)),
            dma((spans, heads, n)),
        ],
        compiler_params=pltpu.CompilerParams(
            collective_id=0, has_side_effects=True, vmem_limit_bytes=60 << 20
        ),
    )(
        visible_blocks,
        block_lists.reshape(-1, slots),
        block_counts,
        queries,
        keys_new,
        values_new,
        key_cache,
        value_cache,
    )


def solution(mesh):
    return jax.shard_map(
        on_device,
        mesh=mesh,
        in_specs=(
            P("section", None, "seq", None),
            P("section", None, "seq", None),
            P("section", None, "seq", None),
            P("section", "seq", None, None),
            P("section", "seq", None, None),
            P("section", "seq", None, None, None),
            P("section", "seq", None, None),
            P(),
        ),
        out_specs=P("section", None, "seq", None),
        check_vma=False,
    )
```

```python
import functools
import math

import jax
import jax.numpy as jnp
from jax import lax
from jax.experimental import pallas as pl
from jax.experimental.pallas import tpu as pltpu
from jax.sharding import PartitionSpec as P

DH = 128
BLK = 64
GROUP = 4
LANES = 128
ROW_TILE = 256
CHUNK = 512
FAR = -1e30


def mesh_copy(src, dst, send_sem, recv_sem, section, seq):
    return pltpu.make_async_remote_copy(
        src_ref=src,
        dst_ref=dst,
        send_sem=send_sem,
        recv_sem=recv_sem,
        device_id=(section, seq),
        device_id_type=pl.DeviceIdType.MESH,
    )


def scores_of(query, keys):
    return lax.dot_general(
        query, keys, (((1,), (1,)), ((), ())), preferred_element_type=jnp.float32
    )


def whole_max(best, scores):
    for i in range(0, scores.shape[1], LANES):
        part = scores[:, i : i + LANES]
        best = part if best is None else jnp.maximum(best, part)
    return best


def fused(
    n,
    sections,
    visible,
    lists,
    counts,
    queries,
    keys_new,
    values_new,
    key_cache,
    value_cache,
    out,
    qbuf,
    kbuf,
    vbuf,
    ckeys,
    cvalues,
    reach,
    att,
    score_buf,
    top_buf,
    in_send,
    in_recv,
    cache_sem,
    out_send,
    out_recv,
    gate,
):
    spans, heads, span_len = qbuf.shape[0], qbuf.shape[1], qbuf.shape[2]
    context = ckeys.shape[1]
    kv_dev = kbuf.shape[1]
    rows = queries.shape[2]
    slots = lists.shape[1]
    query_blocks = span_len // BLK
    items = 2 * kv_dev + heads
    tiles = span_len // ROW_TILE
    columns = reach.shape[1]
    weight_scale = math.log2(math.e) / math.sqrt(DH)
    section = lax.axis_index("section")
    me = lax.axis_index("seq")
    above = lax.rem(section + 1, sections)
    below = lax.rem(section + sections - 1, sections)

    def key_copy(head):
        return pltpu.make_async_copy(key_cache.at[0, head], ckeys.at[head], cache_sem.at[0, head])

    def value_copy(head):
        return pltpu.make_async_copy(
            value_cache.at[0, head], cvalues.at[head], cache_sem.at[1, head]
        )

    def source(span, item, seq):
        if isinstance(item, int) and item < 2 * kv_dev:
            array = keys_new if item < kv_dev else values_new
            column = lax.div(seq * heads, GROUP) * DH + (item % kv_dev) * DH
        else:
            array = queries
            column = (seq * heads + item - 2 * kv_dev) * DH
        return array.at[0, span, :, pl.ds(pl.multiple_of(column, DH), DH)]

    def landing(span, item, seq):
        where = pl.ds(pl.multiple_of(seq * rows, rows), rows)
        if isinstance(item, int) and item < kv_dev:
            return kbuf.at[span, item, where, :]
        if isinstance(item, int) and item < 2 * kv_dev:
            return vbuf.at[span, item - kv_dev, where, :]
        return qbuf.at[span, item - 2 * kv_dev, where, :]

    def own_copy(span, item):
        return pltpu.make_async_copy(
            source(span, item, me), landing(span, item, me), in_recv.at[span, item]
        )

    def in_copy(span, item, k):
        seq_to = lax.rem(me + k, n)
        return mesh_copy(
            source(span, item, seq_to),
            landing(span, item, me),
            in_send.at[span, item],
            in_recv.at[span, item],
            section,
            seq_to,
        )

    def received(span, item, count):
        where = pl.ds(0, count * rows)
        if isinstance(item, int) and item < kv_dev:
            return kbuf.at[span, item, where, :]
        if isinstance(item, int) and item < 2 * kv_dev:
            return vbuf.at[span, item - kv_dev, where, :]
        return qbuf.at[span, item - 2 * kv_dev, where, :]

    def await_in(span, item):
        whole = received(span, item, n)
        pltpu.make_async_copy(whole, whole, in_recv.at[span, item]).wait()

    def await_sent(span, item):
        most = received(span, item, n - 1)
        pltpu.make_async_copy(most, most, in_send.at[span, item]).wait()

    order = [2 * kv_dev] + list(range(2 * kv_dev)) + list(range(2 * kv_dev + 1, items))

    for span in range(spans):
        for item in order:
            own_copy(span, item).start()

    barrier = pltpu.get_barrier_semaphore()

    def greet(k, carry):
        pl.semaphore_signal(
            barrier,
            inc=1,
            device_id=(section, lax.rem(me + k, n)),
            device_id_type=pl.DeviceIdType.MESH,
        )
        return carry

    lax.fori_loop(1, n, greet, 0)
    for there in (above, below):
        pl.semaphore_signal(
            barrier, inc=1, device_id=(there, me), device_id_type=pl.DeviceIdType.MESH
        )
    pl.semaphore_wait(barrier, n + 1)

    for span in range(spans):
        for item in order:

            def send_in(k, carry):
                in_copy(span, item, k).start()
                return carry

            lax.fori_loop(1, n, send_in, 0)

    pl.semaphore_signal(gate, inc=1, device_id=(below, me), device_id_type=pl.DeviceIdType.MESH)

    for head in range(heads):
        key_copy(head).start()
        value_copy(head).start()

    def out_copy(span, head, k):
        seq_to = lax.rem(me + k, n)
        column = pl.multiple_of((me * heads + head) * DH, DH)
        return mesh_copy(
            att.at[span, head, pl.ds(pl.multiple_of(seq_to * rows, rows), rows), :],
            out.at[0, span, :, pl.ds(column, DH)],
            out_send.at[0],
            out_recv.at[0],
            above,
            seq_to,
        )

    def build_reach():
        lane = lax.broadcasted_iota(jnp.int32, (1, columns), 1)
        group = lax.div(lane, query_blocks)
        count = jnp.zeros((1, columns), jnp.float32)
        place = lax.rem(lax.broadcasted_iota(jnp.int32, (query_blocks, columns), 1), query_blocks)
        spread = jnp.where(
            place == lax.broadcasted_iota(jnp.int32, (query_blocks, columns), 0), 1.0, 0.0
        ).astype(jnp.bfloat16)
        span_at = lax.broadcasted_iota(jnp.int32, (spans, columns), 0)
        group_at = lax.div(lax.broadcasted_iota(jnp.int32, (spans, columns), 1), query_blocks)
        for head in range(heads):
            wide = jnp.dot(
                counts[0, head].astype(jnp.float32).astype(jnp.bfloat16),
                spread,
                preferred_element_type=jnp.float32,
            )
            wide = jnp.where(group_at == head * spans + span_at, wide, 0.0)
            count = count + jnp.sum(wide, axis=0, keepdims=True)
        seen = jnp.zeros((1, columns), jnp.int32)
        for span in range(spans):
            seen = jnp.where(lax.rem(group, spans) == span, visible[span], seen)
        seen = seen.astype(jnp.float32)
        eye = jnp.where(
            lax.broadcasted_iota(jnp.int32, (slots, slots), 0)
            == lax.broadcasted_iota(jnp.int32, (slots, slots), 1),
            1.0,
            0.0,
        ).astype(jnp.bfloat16)
        listed = lists[...].astype(jnp.float32)
        if columns > listed.shape[0]:
            listed = jnp.concatenate(
                [listed, jnp.zeros((columns - listed.shape[0], slots), jnp.float32)], axis=0
            )
        listed = scores_of(eye, listed.astype(jnp.bfloat16))
        slot = lax.broadcasted_iota(jnp.int32, (slots, columns), 0).astype(jnp.float32)
        listed = jnp.where((slot < count) & (listed < seen), listed, -1.0)
        blocks = context // BLK
        block = lax.broadcasted_iota(jnp.int32, (blocks, columns), 0).astype(jnp.float32)
        bias = jnp.full((blocks, columns), FAR, jnp.float32)
        for i in range(slots):
            bias = jnp.where(listed[i : i + 1, :] == block, 0.0, bias)
        for j in range(blocks):
            reach[j * BLK : (j + 1) * BLK, :] = jnp.broadcast_to(
                bias[j : j + 1, :], (BLK, columns)
            ).astype(jnp.bfloat16)

    build_reach()
    pl.semaphore_wait(gate, 1)

    row_at = lax.broadcasted_iota(jnp.int32, (ROW_TILE, ROW_TILE), 0)
    key_at = lax.broadcasted_iota(jnp.int32, (ROW_TILE, ROW_TILE), 1)
    mark_row = lax.div(lax.broadcasted_iota(jnp.int32, (ROW_TILE, columns), 0), BLK)
    mark_lane = lax.broadcasted_iota(jnp.int32, (ROW_TILE, columns), 1)

    def score_steps(span, head, kv, tile):
        slot = tile % 2
        at = slice(tile * ROW_TILE, (tile + 1) * ROW_TILE)
        best = [None]
        first = (head * spans + span) * query_blocks + tile * (ROW_TILE // BLK)

        def keep(scores, start):
            score_buf[slot, :, start : start + scores.shape[1]] = scores
            best[0] = whole_max(best[0], scores)

        def cache(start):
            mark = jnp.where(mark_lane == mark_row + first, 1.0, 0.0).astype(jnp.bfloat16)
            query = jnp.concatenate([qbuf[span, head, at, :], mark], axis=1)
            keys = jnp.concatenate(
                [ckeys[head, start : start + CHUNK, :], reach[start : start + CHUNK, :]], axis=1
            )
            keep(scores_of(query, keys), start)

        def own(piece):
            keys = kbuf[span, kv, piece * ROW_TILE : (piece + 1) * ROW_TILE, :]
            scores = scores_of(qbuf[span, head, at, :], keys)
            if piece == tile:
                scores = jnp.where(row_at >= key_at, scores, FAR)
            keep(scores, context + piece * ROW_TILE)

        def finish():
            top = jnp.max(best[0], axis=1, keepdims=True)
            top_buf[slot] = jnp.broadcast_to(top, (ROW_TILE, LANES))

        return (
            [functools.partial(cache, start) for start in range(0, context, CHUNK)]
            + [functools.partial(own, piece) for piece in range(tile + 1)]
            + [finish]
        )

    def value_steps(span, head, kv, tile):
        slot = tile % 2
        total = [None]

        def part(start, values):
            top = top_buf[slot]
            size = values.shape[0]
            weights = []
            for i in range(start, start + size, LANES):
                scores = score_buf[slot, :, i : i + LANES]
                weights.append(jnp.exp2((scores - top) * weight_scale).astype(jnp.bfloat16))
            values = jnp.concatenate([values, jnp.ones((size, LANES), jnp.bfloat16)], axis=1)
            product = jnp.dot(
                jnp.concatenate(weights, axis=1), values, preferred_element_type=jnp.float32
            )
            total[0] = product if total[0] is None else total[0] + product

        def cache(start):
            part(start, cvalues[head, start : start + CHUNK, :])

        def own(piece):
            part(
                context + piece * ROW_TILE,
                vbuf[span, kv, piece * ROW_TILE : (piece + 1) * ROW_TILE, :],
            )

        def finish():
            mixed = total[0][:, :DH] / total[0][:, DH:]
            att[span, head, tile * ROW_TILE : (tile + 1) * ROW_TILE, :] = mixed.astype(
                jnp.bfloat16
            )

        return (
            [functools.partial(cache, start) for start in range(0, context, CHUNK)]
            + [functools.partial(own, piece) for piece in range(tile + 1)]
            + [finish]
        )

    def one_unit(unit, carry):
        span, head = lax.div(unit, heads), lax.rem(unit, heads)
        kv = lax.div(head, GROUP)

        @pl.when(head == 0)
        def _():
            for item in range(2 * kv_dev):
                await_in(span, item)

        @pl.when(span == 0)
        def _():
            key_copy(head).wait()
            value_copy(head).wait()

        await_in(span, 2 * kv_dev + head)
        for step in score_steps(span, head, kv, 0):
            step()
        for tile in range(tiles):
            now = value_steps(span, head, kv, tile)
            later = score_steps(span, head, kv, tile + 1) if tile + 1 < tiles else []
            for i in range(max(len(now), len(later))):
                if i < len(later):
                    later[i]()
                if i < len(now):
                    now[i]()

        def send_out(k, inner):
            out_copy(span, head, k).start()
            return inner

        lax.fori_loop(0, n, send_out, 0)
        return carry

    lax.fori_loop(0, spans * heads, one_unit, 0)

    for span in range(spans):
        for item in range(items):
            await_sent(span, item)
    pltpu.make_async_copy(att, att, out_send.at[0]).wait()
    pltpu.make_async_copy(out, out, out_recv.at[0]).wait()


def on_device(
    queries, keys_new, values_new, key_cache, value_cache, block_lists, block_counts, visible_blocks
):
    n = lax.axis_size("seq")
    sections = lax.axis_size("section")
    spans, rows = queries.shape[1], queries.shape[2]
    heads, context = key_cache.shape[1], key_cache.shape[2]
    kv_dev = max(1, heads // GROUP)
    span_len = rows * n
    items = 2 * kv_dev + heads
    slots = block_lists.shape[4]
    smem = pl.BlockSpec(memory_space=pltpu.MemorySpace.SMEM)
    vmem = pl.BlockSpec(memory_space=pltpu.MemorySpace.VMEM)
    anywhere = pl.BlockSpec(memory_space=pl.ANY)
    cols = -(-heads * spans * (span_len // BLK) // LANES) * LANES
    dma = pltpu.SemaphoreType.DMA
    return pl.pallas_call(
        functools.partial(fused, n, sections),
        out_shape=pltpu.VMEM(queries.shape, queries.dtype),
        in_specs=[smem, vmem, vmem] + [anywhere] * 5,
        out_specs=vmem,
        scratch_shapes=[
            pltpu.VMEM((spans, heads, span_len, DH), jnp.bfloat16),
            pltpu.VMEM((spans, kv_dev, span_len, DH), jnp.bfloat16),
            pltpu.VMEM((spans, kv_dev, span_len, DH), jnp.bfloat16),
            pltpu.VMEM((heads, context, DH), jnp.bfloat16),
            pltpu.VMEM((heads, context, DH), jnp.bfloat16),
            pltpu.VMEM((context, cols), jnp.bfloat16),
            pltpu.VMEM((spans, heads, span_len, DH), jnp.bfloat16),
            pltpu.VMEM((2, ROW_TILE, context + span_len), jnp.float32),
            pltpu.VMEM((2, ROW_TILE, LANES), jnp.float32),
            dma((spans, items)),
            dma((spans, items)),
            dma((2, heads)),
            dma((1,)),
            dma((1,)),
            pltpu.SemaphoreType.REGULAR,
        ],
        compiler_params=pltpu.CompilerParams(
            collective_id=0, has_side_effects=True, vmem_limit_bytes=60 << 20
        ),
    )(
        visible_blocks,
        block_lists.reshape(-1, slots),
        block_counts,
        queries,
        keys_new,
        values_new,
        key_cache,
        value_cache,
    )


def solution(mesh):
    return jax.shard_map(
        on_device,
        mesh=mesh,
        in_specs=(
            P("section", None, "seq", None),
            P("section", None, "seq", None),
            P("section", None, "seq", None),
            P("section", "seq", None, None),
            P("section", "seq", None, None),
            P("section", "seq", None, None, None),
            P("section", "seq", None, None),
            P(),
        ),
        out_specs=P("section", None, "seq", None),
        check_vma=False,
    )
```

```python
import functools
import math

import jax
import jax.numpy as jnp
from jax import lax
from jax.experimental import pallas as pl
from jax.experimental.pallas import tpu as pltpu
from jax.sharding import PartitionSpec as P

DH = 128
BLK = 64
GROUP = 4
LANES = 128
ROW_TILE = 256
CHUNK = 512
FAR = -1e30
DIRECT = 4
LAG = 3


def mesh_copy(src, dst, send_sem, recv_sem, section, seq):
    return pltpu.make_async_remote_copy(
        src_ref=src,
        dst_ref=dst,
        send_sem=send_sem,
        recv_sem=recv_sem,
        device_id=(section, seq),
        device_id_type=pl.DeviceIdType.MESH,
    )


def scores_of(query, keys):
    return lax.dot_general(
        query, keys, (((1,), (1,)), ((), ())), preferred_element_type=jnp.float32
    )


def whole_max(best, scores):
    for i in range(0, scores.shape[1], LANES):
        part = scores[:, i : i + LANES]
        best = part if best is None else jnp.maximum(best, part)
    return best


def fused(
    n,
    sections,
    visible,
    lists,
    counts,
    queries,
    keys_new,
    values_new,
    key_cache,
    value_cache,
    out,
    qbuf,
    kbuf,
    vbuf,
    ckeys,
    cvalues,
    reach,
    att,
    score_buf,
    top_buf,
    in_send,
    in_recv,
    cache_sem,
    out_send,
    out_recv,
    stage,
    stage_recv,
    pass_send,
    gate,
):
    spans, heads, span_len = qbuf.shape[0], qbuf.shape[1], qbuf.shape[2]
    context = ckeys.shape[1]
    kv_dev = kbuf.shape[1]
    rows = queries.shape[2]
    slots = lists.shape[1]
    query_blocks = span_len // BLK
    items = 2 * kv_dev + heads
    tiles = span_len // ROW_TILE
    columns = reach.shape[1]
    weight_scale = math.log2(math.e) / math.sqrt(DH)
    section = lax.axis_index("section")
    me = lax.axis_index("seq")
    above = lax.rem(section + 1, sections)
    below = lax.rem(section + sections - 1, sections)

    def key_copy(head):
        return pltpu.make_async_copy(key_cache.at[0, head], ckeys.at[head], cache_sem.at[0, head])

    def value_copy(head):
        return pltpu.make_async_copy(
            value_cache.at[0, head], cvalues.at[head], cache_sem.at[1, head]
        )

    def source(span, item, seq):
        if isinstance(item, int) and item < 2 * kv_dev:
            array = keys_new if item < kv_dev else values_new
            column = lax.div(seq * heads, GROUP) * DH + (item % kv_dev) * DH
        else:
            array = queries
            column = (seq * heads + item - 2 * kv_dev) * DH
        return array.at[0, span, :, pl.ds(pl.multiple_of(column, DH), DH)]

    def landing(span, item, seq):
        where = pl.ds(pl.multiple_of(seq * rows, rows), rows)
        if isinstance(item, int) and item < kv_dev:
            return kbuf.at[span, item, where, :]
        if isinstance(item, int) and item < 2 * kv_dev:
            return vbuf.at[span, item - kv_dev, where, :]
        return qbuf.at[span, item - 2 * kv_dev, where, :]

    def own_copy(span, item):
        return pltpu.make_async_copy(
            source(span, item, me), landing(span, item, me), in_recv.at[span, item]
        )

    def in_copy(span, item, k):
        seq_to = lax.rem(me + k, n)
        return mesh_copy(
            source(span, item, seq_to),
            landing(span, item, me),
            in_send.at[span, item],
            in_recv.at[span, item],
            section,
            seq_to,
        )

    def received(span, item, count):
        where = pl.ds(0, count * rows)
        if isinstance(item, int) and item < kv_dev:
            return kbuf.at[span, item, where, :]
        if isinstance(item, int) and item < 2 * kv_dev:
            return vbuf.at[span, item - kv_dev, where, :]
        return qbuf.at[span, item - 2 * kv_dev, where, :]

    def await_in(span, item):
        whole = received(span, item, n)
        pltpu.make_async_copy(whole, whole, in_recv.at[span, item]).wait()

    def await_sent(span, item):
        most = received(span, item, n - 1)
        pltpu.make_async_copy(most, most, in_send.at[span, item]).wait()

    order = [2 * kv_dev] + list(range(2 * kv_dev)) + list(range(2 * kv_dev + 1, items))

    for span in range(spans):
        for item in order:
            own_copy(span, item).start()

    barrier = pltpu.get_barrier_semaphore()

    def greet(k, carry):
        pl.semaphore_signal(
            barrier,
            inc=1,
            device_id=(section, lax.rem(me + k, n)),
            device_id_type=pl.DeviceIdType.MESH,
        )
        return carry

    lax.fori_loop(1, n, greet, 0)
    for there in (above, below):
        pl.semaphore_signal(
            barrier, inc=1, device_id=(there, me), device_id_type=pl.DeviceIdType.MESH
        )
    pl.semaphore_wait(barrier, n + 1)

    for span in range(spans):
        for item in order:

            def send_in(k, carry):
                in_copy(span, item, k).start()
                return carry

            lax.fori_loop(1, n, send_in, 0)

    pl.semaphore_signal(gate, inc=1, device_id=(below, me), device_id_type=pl.DeviceIdType.MESH)

    for head in range(heads):
        key_copy(head).start()
        value_copy(head).start()

    units = spans * heads
    relayed = max(0, units - DIRECT)

    def out_piece(buffer, span, head, seq_from, seq_to):
        column = pl.multiple_of((seq_from * heads + head) * DH, DH)
        where = pl.ds(pl.multiple_of(seq_to * rows, rows), rows)
        return buffer.at[where, :], out.at[0, span, :, pl.ds(column, DH)]

    def out_copy(span, head, k):
        seq_to = lax.rem(me + k, n)
        source_ref, target_ref = out_piece(att.at[span, head], span, head, me, seq_to)
        return mesh_copy(source_ref, target_ref, out_send.at[0], out_recv.at[0], above, seq_to)

    def up_copy(span, head, tile):
        where = pl.ds(tile * ROW_TILE, ROW_TILE)
        unit = span * heads + head
        return mesh_copy(
            att.at[span, head, where, :],
            stage.at[unit, where, :],
            out_send.at[0],
            stage_recv.at[unit],
            above,
            me,
        )

    def pass_on(unit):
        span, head = unit // heads, unit % heads
        whole = stage.at[unit]
        pltpu.make_async_copy(whole, whole, stage_recv.at[unit]).wait()
        source_ref, target_ref = out_piece(whole, span, head, me, me)
        pltpu.make_async_copy(source_ref, target_ref, out_recv.at[0]).start()

        def one(k, carry):
            seq_to = lax.rem(me + k, n)
            source_ref, target_ref = out_piece(whole, span, head, me, seq_to)
            mesh_copy(
                source_ref, target_ref, pass_send.at[0], out_recv.at[0], section, seq_to
            ).start()
            return carry

        lax.fori_loop(1, n, one, 0)

    def pass_after(unit):
        return max(unit + LAG, units // 2 - 1 + (unit > 0))

    def build_reach():
        lane = lax.broadcasted_iota(jnp.int32, (1, columns), 1)
        group = lax.div(lane, query_blocks)
        count = jnp.zeros((1, columns), jnp.float32)
        place = lax.rem(lax.broadcasted_iota(jnp.int32, (query_blocks, columns), 1), query_blocks)
        spread = jnp.where(
            place == lax.broadcasted_iota(jnp.int32, (query_blocks, columns), 0), 1.0, 0.0
        ).astype(jnp.bfloat16)
        span_at = lax.broadcasted_iota(jnp.int32, (spans, columns), 0)
        group_at = lax.div(lax.broadcasted_iota(jnp.int32, (spans, columns), 1), query_blocks)
        for head in range(heads):
            wide = jnp.dot(
                counts[0, head].astype(jnp.float32).astype(jnp.bfloat16),
                spread,
                preferred_element_type=jnp.float32,
            )
            wide = jnp.where(group_at == head * spans + span_at, wide, 0.0)
            count = count + jnp.sum(wide, axis=0, keepdims=True)
        seen = jnp.zeros((1, columns), jnp.int32)
        for span in range(spans):
            seen = jnp.where(lax.rem(group, spans) == span, visible[span], seen)
        seen = seen.astype(jnp.float32)
        eye = jnp.where(
            lax.broadcasted_iota(jnp.int32, (slots, slots), 0)
            == lax.broadcasted_iota(jnp.int32, (slots, slots), 1),
            1.0,
            0.0,
        ).astype(jnp.bfloat16)
        listed = lists[...].astype(jnp.float32)
        if columns > listed.shape[0]:
            listed = jnp.concatenate(
                [listed, jnp.zeros((columns - listed.shape[0], slots), jnp.float32)], axis=0
            )
        listed = scores_of(eye, listed.astype(jnp.bfloat16))
        slot = lax.broadcasted_iota(jnp.int32, (slots, columns), 0).astype(jnp.float32)
        listed = jnp.where((slot < count) & (listed < seen), listed, -1.0)
        blocks = context // BLK
        block = lax.broadcasted_iota(jnp.int32, (blocks, columns), 0).astype(jnp.float32)
        bias = jnp.full((blocks, columns), FAR, jnp.float32)
        for i in range(slots):
            bias = jnp.where(listed[i : i + 1, :] == block, 0.0, bias)
        for j in range(blocks):
            reach[j * BLK : (j + 1) * BLK, :] = jnp.broadcast_to(
                bias[j : j + 1, :], (BLK, columns)
            ).astype(jnp.bfloat16)

    build_reach()
    pl.semaphore_wait(gate, 1)

    row_at = lax.broadcasted_iota(jnp.int32, (ROW_TILE, ROW_TILE), 0)
    key_at = lax.broadcasted_iota(jnp.int32, (ROW_TILE, ROW_TILE), 1)
    mark_row = lax.div(lax.broadcasted_iota(jnp.int32, (ROW_TILE, columns), 0), BLK)
    mark_lane = lax.broadcasted_iota(jnp.int32, (ROW_TILE, columns), 1)

    def score_steps(span, head, kv, tile):
        slot = tile % 2
        at = slice(tile * ROW_TILE, (tile + 1) * ROW_TILE)
        best = [None]
        first = (head * spans + span) * query_blocks + tile * (ROW_TILE // BLK)

        def keep(scores, start):
            score_buf[slot, :, start : start + scores.shape[1]] = scores
            best[0] = whole_max(best[0], scores)

        def cache(start):
            mark = jnp.where(mark_lane == mark_row + first, 1.0, 0.0).astype(jnp.bfloat16)
            query = jnp.concatenate([qbuf[span, head, at, :], mark], axis=1)
            keys = jnp.concatenate(
                [ckeys[head, start : start + CHUNK, :], reach[start : start + CHUNK, :]], axis=1
            )
            keep(scores_of(query, keys), start)

        def own(piece):
            keys = kbuf[span, kv, piece * ROW_TILE : (piece + 1) * ROW_TILE, :]
            scores = scores_of(qbuf[span, head, at, :], keys)
            if piece == tile:
                scores = jnp.where(row_at >= key_at, scores, FAR)
            keep(scores, context + piece * ROW_TILE)

        def finish():
            top = jnp.max(best[0], axis=1, keepdims=True)
            top_buf[slot] = jnp.broadcast_to(top, (ROW_TILE, LANES))

        return (
            [functools.partial(cache, start) for start in range(0, context, CHUNK)]
            + [functools.partial(own, piece) for piece in range(tile + 1)]
            + [finish]
        )

    def value_steps(span, head, kv, tile):
        slot = tile % 2
        total = [None]

        def part(start, values):
            top = top_buf[slot]
            size = values.shape[0]
            weights = []
            for i in range(start, start + size, LANES):
                scores = score_buf[slot, :, i : i + LANES]
                weights.append(jnp.exp2((scores - top) * weight_scale).astype(jnp.bfloat16))
            values = jnp.concatenate([values, jnp.ones((size, LANES), jnp.bfloat16)], axis=1)
            product = jnp.dot(
                jnp.concatenate(weights, axis=1), values, preferred_element_type=jnp.float32
            )
            total[0] = product if total[0] is None else total[0] + product

        def cache(start):
            part(start, cvalues[head, start : start + CHUNK, :])

        def own(piece):
            part(
                context + piece * ROW_TILE,
                vbuf[span, kv, piece * ROW_TILE : (piece + 1) * ROW_TILE, :],
            )

        def finish():
            mixed = total[0][:, :DH] / total[0][:, DH:]
            att[span, head, tile * ROW_TILE : (tile + 1) * ROW_TILE, :] = mixed.astype(
                jnp.bfloat16
            )

        return (
            [functools.partial(cache, start) for start in range(0, context, CHUNK)]
            + [functools.partial(own, piece) for piece in range(tile + 1)]
            + [finish]
        )

    def one_unit(unit, carry):
        span, head = lax.div(unit, heads), lax.rem(unit, heads)
        kv = lax.div(head, GROUP)

        @pl.when(head == 0)
        def _():
            for item in range(2 * kv_dev):
                await_in(span, item)

        @pl.when(span == 0)
        def _():
            key_copy(head).wait()
            value_copy(head).wait()

        await_in(span, 2 * kv_dev + head)
        for step in score_steps(span, head, kv, 0):
            step()
        for tile in range(tiles):
            now = value_steps(span, head, kv, tile)
            later = score_steps(span, head, kv, tile + 1) if tile + 1 < tiles else []
            for i in range(max(len(now), len(later))):
                if i < len(later):
                    later[i]()
                if i < len(now):
                    now[i]()


        @pl.when(unit < relayed)
        def _():
            for tile in range(tiles):
                up_copy(span, head, tile).start()

        @pl.when(unit >= relayed)
        def _():
            def send_out(k, inner):
                out_copy(span, head, k).start()
                return inner

            lax.fori_loop(0, n, send_out, 0)

        for done in range(relayed):

            @pl.when(unit == pass_after(done))
            def _():
                pass_on(done)

        return carry

    lax.fori_loop(0, units, one_unit, 0)
    for done in range(relayed):
        if pass_after(done) >= units:
            pass_on(done)

    for span in range(spans):
        for item in range(items):
            await_sent(span, item)
    pltpu.make_async_copy(att, att, out_send.at[0]).wait()
    if relayed:
        passed = stage.at[:, pl.ds(0, (n - 1) * rows), :]
        pltpu.make_async_copy(passed, passed, pass_send.at[0]).wait()
    pltpu.make_async_copy(out, out, out_recv.at[0]).wait()


def on_device(
    queries, keys_new, values_new, key_cache, value_cache, block_lists, block_counts, visible_blocks
):
    n = lax.axis_size("seq")
    sections = lax.axis_size("section")
    spans, rows = queries.shape[1], queries.shape[2]
    heads, context = key_cache.shape[1], key_cache.shape[2]
    kv_dev = max(1, heads // GROUP)
    span_len = rows * n
    items = 2 * kv_dev + heads
    slots = block_lists.shape[4]
    smem = pl.BlockSpec(memory_space=pltpu.MemorySpace.SMEM)
    vmem = pl.BlockSpec(memory_space=pltpu.MemorySpace.VMEM)
    anywhere = pl.BlockSpec(memory_space=pl.ANY)
    relayed = max(0, spans * heads - DIRECT)
    cols = -(-heads * spans * (span_len // BLK) // LANES) * LANES
    dma = pltpu.SemaphoreType.DMA
    return pl.pallas_call(
        functools.partial(fused, n, sections),
        out_shape=pltpu.VMEM(queries.shape, queries.dtype),
        in_specs=[smem, vmem, vmem] + [anywhere] * 5,
        out_specs=vmem,
        scratch_shapes=[
            pltpu.VMEM((spans, heads, span_len, DH), jnp.bfloat16),
            pltpu.VMEM((spans, kv_dev, span_len, DH), jnp.bfloat16),
            pltpu.VMEM((spans, kv_dev, span_len, DH), jnp.bfloat16),
            pltpu.VMEM((heads, context, DH), jnp.bfloat16),
            pltpu.VMEM((heads, context, DH), jnp.bfloat16),
            pltpu.VMEM((context, cols), jnp.bfloat16),
            pltpu.VMEM((spans, heads, span_len, DH), jnp.bfloat16),
            pltpu.VMEM((2, ROW_TILE, context + span_len), jnp.float32),
            pltpu.VMEM((2, ROW_TILE, LANES), jnp.float32),
            dma((spans, items)),
            dma((spans, items)),
            dma((2, heads)),
            dma((1,)),
            dma((1,)),
            pltpu.VMEM((relayed, span_len, DH), jnp.bfloat16),
            dma((relayed,)),
            dma((1,)),
            pltpu.SemaphoreType.REGULAR,
        ],
        compiler_params=pltpu.CompilerParams(
            collective_id=0, has_side_effects=True, vmem_limit_bytes=60 << 20
        ),
    )(
        visible_blocks,
        block_lists.reshape(-1, slots),
        block_counts,
        queries,
        keys_new,
        values_new,
        key_cache,
        value_cache,
    )


def solution(mesh):
    return jax.shard_map(
        on_device,
        mesh=mesh,
        in_specs=(
            P("section", None, "seq", None),
            P("section", None, "seq", None),
            P("section", None, "seq", None),
            P("section", "seq", None, None),
            P("section", "seq", None, None),
            P("section", "seq", None, None, None),
            P("section", "seq", None, None),
            P(),
        ),
        out_specs=P("section", None, "seq", None),
        check_vma=False,
    )
```

```python
import functools
import math

import jax
import jax.numpy as jnp
from jax import lax
from jax.experimental import pallas as pl
from jax.experimental.pallas import tpu as pltpu
from jax.sharding import PartitionSpec as P

DH = 128
BLK = 64
GROUP = 4
LANES = 128
ROW_TILE = 256
CHUNK = 512
FAR = -1e30
DIRECT = 4
LAG = 3


def mesh_copy(src, dst, send_sem, recv_sem, section, seq):
    return pltpu.make_async_remote_copy(
        src_ref=src,
        dst_ref=dst,
        send_sem=send_sem,
        recv_sem=recv_sem,
        device_id=(section, seq),
        device_id_type=pl.DeviceIdType.MESH,
    )


def scores_of(query, keys):
    return lax.dot_general(
        query, keys, (((1,), (1,)), ((), ())), preferred_element_type=jnp.float32
    )


def whole_max(best, scores):
    for i in range(0, scores.shape[1], LANES):
        part = scores[:, i : i + LANES]
        best = part if best is None else jnp.maximum(best, part)
    return best


def fused(
    n,
    sections,
    visible,
    lists,
    counts,
    queries,
    keys_new,
    values_new,
    key_cache,
    value_cache,
    out,
    qbuf,
    kbuf,
    vbuf,
    ckeys,
    cvalues,
    reach,
    att,
    score_buf,
    top_buf,
    in_send,
    in_recv,
    cache_sem,
    out_send,
    out_recv,
    stage,
    stage_recv,
    pass_send,
    gate,
):
    spans, heads, span_len = qbuf.shape[0], qbuf.shape[1], qbuf.shape[2]
    context = ckeys.shape[1]
    kv_dev = kbuf.shape[1]
    rows = queries.shape[2]
    slots = lists.shape[1]
    query_blocks = span_len // BLK
    items = 2 * kv_dev + heads
    tiles = span_len // ROW_TILE
    columns = reach.shape[1]
    weight_scale = math.log2(math.e) / math.sqrt(DH)
    section = lax.axis_index("section")
    me = lax.axis_index("seq")
    above = lax.rem(section + 1, sections)
    below = lax.rem(section + sections - 1, sections)

    def key_copy(head):
        return pltpu.make_async_copy(key_cache.at[0, head], ckeys.at[head], cache_sem.at[0, head])

    def value_copy(head):
        return pltpu.make_async_copy(
            value_cache.at[0, head], cvalues.at[head], cache_sem.at[1, head]
        )

    def source(span, item, seq):
        if isinstance(item, int) and item < 2 * kv_dev:
            array = keys_new if item < kv_dev else values_new
            column = lax.div(seq * heads, GROUP) * DH + (item % kv_dev) * DH
        else:
            array = queries
            column = (seq * heads + item - 2 * kv_dev) * DH
        return array.at[0, span, :, pl.ds(pl.multiple_of(column, DH), DH)]

    def landing(span, item, seq):
        where = pl.ds(pl.multiple_of(seq * rows, rows), rows)
        if isinstance(item, int) and item < kv_dev:
            return kbuf.at[span, item, where, :]
        if isinstance(item, int) and item < 2 * kv_dev:
            return vbuf.at[span, item - kv_dev, where, :]
        return qbuf.at[span, item - 2 * kv_dev, where, :]

    def own_copy(span, item):
        return pltpu.make_async_copy(
            source(span, item, me), landing(span, item, me), in_recv.at[span, item]
        )

    def in_copy(span, item, k):
        seq_to = lax.rem(me + k, n)
        return mesh_copy(
            source(span, item, seq_to),
            landing(span, item, me),
            in_send.at[span, item],
            in_recv.at[span, item],
            section,
            seq_to,
        )

    def received(span, item, count):
        where = pl.ds(0, count * rows)
        if isinstance(item, int) and item < kv_dev:
            return kbuf.at[span, item, where, :]
        if isinstance(item, int) and item < 2 * kv_dev:
            return vbuf.at[span, item - kv_dev, where, :]
        return qbuf.at[span, item - 2 * kv_dev, where, :]

    def await_in(span, item):
        whole = received(span, item, n)
        pltpu.make_async_copy(whole, whole, in_recv.at[span, item]).wait()

    def await_sent(span, item):
        most = received(span, item, n - 1)
        pltpu.make_async_copy(most, most, in_send.at[span, item]).wait()

    order = [2 * kv_dev] + list(range(2 * kv_dev)) + list(range(2 * kv_dev + 1, items))

    barrier = pltpu.get_barrier_semaphore()

    def greet(k, carry):
        pl.semaphore_signal(
            barrier,
            inc=1,
            device_id=(section, lax.rem(me + k, n)),
            device_id_type=pl.DeviceIdType.MESH,
        )
        return carry

    lax.fori_loop(1, n, greet, 0)
    for there in (above, below):
        pl.semaphore_signal(
            barrier, inc=1, device_id=(there, me), device_id_type=pl.DeviceIdType.MESH
        )
    pl.semaphore_wait(barrier, n + 1)

    def send_items(span, some):
        for item in some:

            def send_in(k, carry):
                in_copy(span, item, k).start()
                return carry

            lax.fori_loop(1, n, send_in, 0)
        for item in some:
            own_copy(span, item).start()

    urgent = 1 + 2 * kv_dev
    send_items(0, order[:urgent])

    pl.semaphore_signal(gate, inc=1, device_id=(below, me), device_id_type=pl.DeviceIdType.MESH)

    for head in range(heads):
        key_copy(head).start()
        value_copy(head).start()

    units = spans * heads
    relayed = max(1, units - DIRECT)

    def out_piece(buffer, span, head, seq_from, seq_to):
        column = pl.multiple_of((seq_from * heads + head) * DH, DH)
        where = pl.ds(pl.multiple_of(seq_to * rows, rows), rows)
        return buffer.at[where, :], out.at[0, span, :, pl.ds(column, DH)]

    def out_copy(span, head, k):
        seq_to = lax.rem(me + k, n)
        source_ref, target_ref = out_piece(att.at[span, head], span, head, me, seq_to)
        return mesh_copy(source_ref, target_ref, out_send.at[0], out_recv.at[0], above, seq_to)

    def up_copy(span, head, tile):
        where = pl.ds(tile * ROW_TILE, ROW_TILE)
        unit = span * heads + head
        return mesh_copy(
            att.at[span, head, where, :],
            stage.at[unit, where, :],
            out_send.at[0],
            stage_recv.at[unit],
            above,
            me,
        )

    def pass_on(unit):
        span, head = unit // heads, unit % heads
        whole = stage.at[unit]
        pltpu.make_async_copy(whole, whole, stage_recv.at[unit]).wait()
        source_ref, target_ref = out_piece(whole, span, head, me, me)
        pltpu.make_async_copy(source_ref, target_ref, out_recv.at[0]).start()

        def one(k, carry):
            seq_to = lax.rem(me + k, n)
            source_ref, target_ref = out_piece(whole, span, head, me, seq_to)
            mesh_copy(
                source_ref, target_ref, pass_send.at[0], out_recv.at[0], section, seq_to
            ).start()
            return carry

        lax.fori_loop(1, n, one, 0)

    def pass_after(unit):
        return max(1, unit + LAG, units // 2 - 1 + (unit > 0))

    def build_reach():
        lane = lax.broadcasted_iota(jnp.int32, (1, columns), 1)
        group = lax.div(lane, query_blocks)
        count = jnp.zeros((1, columns), jnp.float32)
        place = lax.rem(lax.broadcasted_iota(jnp.int32, (query_blocks, columns), 1), query_blocks)
        spread = jnp.where(
            place == lax.broadcasted_iota(jnp.int32, (query_blocks, columns), 0), 1.0, 0.0
        ).astype(jnp.bfloat16)
        span_at = lax.broadcasted_iota(jnp.int32, (spans, columns), 0)
        group_at = lax.div(lax.broadcasted_iota(jnp.int32, (spans, columns), 1), query_blocks)
        for head in range(heads):
            wide = jnp.dot(
                counts[0, head].astype(jnp.float32).astype(jnp.bfloat16),
                spread,
                preferred_element_type=jnp.float32,
            )
            wide = jnp.where(group_at == head * spans + span_at, wide, 0.0)
            count = count + jnp.sum(wide, axis=0, keepdims=True)
        seen = jnp.zeros((1, columns), jnp.int32)
        for span in range(spans):
            seen = jnp.where(lax.rem(group, spans) == span, visible[span], seen)
        seen = seen.astype(jnp.float32)
        eye = jnp.where(
            lax.broadcasted_iota(jnp.int32, (slots, slots), 0)
            == lax.broadcasted_iota(jnp.int32, (slots, slots), 1),
            1.0,
            0.0,
        ).astype(jnp.bfloat16)
        listed = lists[...].astype(jnp.float32)
        if columns > listed.shape[0]:
            listed = jnp.concatenate(
                [listed, jnp.zeros((columns - listed.shape[0], slots), jnp.float32)], axis=0
            )
        listed = scores_of(eye, listed.astype(jnp.bfloat16))
        slot = lax.broadcasted_iota(jnp.int32, (slots, columns), 0).astype(jnp.float32)
        listed = jnp.where((slot < count) & (listed < seen), listed, -1.0)
        blocks = context // BLK
        block = lax.broadcasted_iota(jnp.int32, (blocks, columns), 0).astype(jnp.float32)
        bias = jnp.full((blocks, columns), FAR, jnp.float32)
        for i in range(slots):
            bias = jnp.where(listed[i : i + 1, :] == block, 0.0, bias)
        for j in range(blocks):
            reach[j * BLK : (j + 1) * BLK, :] = jnp.broadcast_to(
                bias[j : j + 1, :], (BLK, columns)
            ).astype(jnp.bfloat16)

    build_reach()
    pl.semaphore_wait(gate, 1)

    row_at = lax.broadcasted_iota(jnp.int32, (ROW_TILE, ROW_TILE), 0)
    key_at = lax.broadcasted_iota(jnp.int32, (ROW_TILE, ROW_TILE), 1)
    mark_row = lax.div(lax.broadcasted_iota(jnp.int32, (ROW_TILE, columns), 0), BLK)
    mark_lane = lax.broadcasted_iota(jnp.int32, (ROW_TILE, columns), 1)

    def score_steps(span, head, kv, tile):
        slot = tile
        at = slice(tile * ROW_TILE, (tile + 1) * ROW_TILE)
        best = [None]
        first = (head * spans + span) * query_blocks + tile * (ROW_TILE // BLK)

        def keep(scores, start):
            score_buf[slot, :, start : start + scores.shape[1]] = scores
            best[0] = whole_max(best[0], scores)

        def cache(start):
            mark = jnp.where(mark_lane == mark_row + first, 1.0, 0.0).astype(jnp.bfloat16)
            query = jnp.concatenate([qbuf[span, head, at, :], mark], axis=1)
            keys = jnp.concatenate(
                [ckeys[head, start : start + CHUNK, :], reach[start : start + CHUNK, :]], axis=1
            )
            keep(scores_of(query, keys), start)

        def own(piece):
            keys = kbuf[span, kv, piece * ROW_TILE : (piece + 1) * ROW_TILE, :]
            scores = scores_of(qbuf[span, head, at, :], keys)
            if piece == tile:
                scores = jnp.where(row_at >= key_at, scores, FAR)
            keep(scores, context + piece * ROW_TILE)

        def finish():
            top = jnp.max(best[0], axis=1, keepdims=True)
            top_buf[slot] = jnp.broadcast_to(top, (ROW_TILE, LANES))

        return (
            [functools.partial(cache, start) for start in range(0, context, CHUNK)],
            [functools.partial(own, piece) for piece in range(tile + 1)] + [finish],
        )

    def value_steps(span, head, kv, tile):
        slot = tile
        total = [None]

        def part(start, values):
            top = top_buf[slot]
            size = values.shape[0]
            weights = []
            for i in range(start, start + size, LANES):
                scores = score_buf[slot, :, i : i + LANES]
                weights.append(jnp.exp2((scores - top) * weight_scale).astype(jnp.bfloat16))
            values = jnp.concatenate([values, jnp.ones((size, LANES), jnp.bfloat16)], axis=1)
            product = jnp.dot(
                jnp.concatenate(weights, axis=1), values, preferred_element_type=jnp.float32
            )
            total[0] = product if total[0] is None else total[0] + product

        def cache(start):
            part(start, cvalues[head, start : start + CHUNK, :])

        def own(piece):
            part(
                context + piece * ROW_TILE,
                vbuf[span, kv, piece * ROW_TILE : (piece + 1) * ROW_TILE, :],
            )

        def finish():
            mixed = total[0][:, :DH] / total[0][:, DH:]
            att[span, head, tile * ROW_TILE : (tile + 1) * ROW_TILE, :] = mixed.astype(
                jnp.bfloat16
            )

        return (
            [functools.partial(cache, start) for start in range(0, context, CHUNK)]
            + [functools.partial(own, piece) for piece in range(tile + 1)]
            + [finish]
        )

    def together(first, second):
        for i in range(max(len(first), len(second))):
            if i < len(first):
                first[i]()
            if i < len(second):
                second[i]()

    def first_unit():
        key_copy(0).wait()
        value_copy(0).wait()
        await_in(0, 2 * kv_dev)
        steps = [score_steps(0, 0, 0, tile) for tile in range(tiles)]
        for cached, _ in steps:
            for step in cached:
                step()
        send_items(0, order[urgent:])
        for span in range(1, spans):
            send_items(span, order)
        for item in range(2 * kv_dev):
            await_in(0, item)
        for step in steps[0][1]:
            step()
        for tile in range(tiles):
            later = steps[tile + 1][1] if tile + 1 < tiles else []
            together(later, value_steps(0, 0, 0, tile))
        for tile in range(tiles):
            up_copy(0, 0, tile).start()

    def one_unit(unit, carry):
        span, head = lax.div(unit, heads), lax.rem(unit, heads)
        kv = lax.div(head, GROUP)

        @pl.when(head == 0)
        def _():
            for item in range(2 * kv_dev):
                await_in(span, item)

        @pl.when(span == 0)
        def _():
            key_copy(head).wait()
            value_copy(head).wait()

        await_in(span, 2 * kv_dev + head)
        for steps in score_steps(span, head, kv, 0):
            for step in steps:
                step()
        for tile in range(tiles):
            later = []
            if tile + 1 < tiles:
                later = sum(score_steps(span, head, kv, tile + 1), [])
            together(later, value_steps(span, head, kv, tile))

        @pl.when(unit < relayed)
        def _():
            for tile in range(tiles):
                up_copy(span, head, tile).start()

        @pl.when(unit >= relayed)
        def _():
            def send_out(k, inner):
                out_copy(span, head, k).start()
                return inner

            lax.fori_loop(0, n, send_out, 0)

        for done in range(relayed):

            @pl.when(unit == pass_after(done))
            def _():
                pass_on(done)

        return carry

    first_unit()
    lax.fori_loop(1, units, one_unit, 0)
    for done in range(relayed):
        if pass_after(done) >= units:
            pass_on(done)

    for span in range(spans):
        for item in range(items):
            await_sent(span, item)
    pltpu.make_async_copy(att, att, out_send.at[0]).wait()
    passed = stage.at[:, pl.ds(0, (n - 1) * rows), :]
    pltpu.make_async_copy(passed, passed, pass_send.at[0]).wait()
    pltpu.make_async_copy(out, out, out_recv.at[0]).wait()


def on_device(
    queries, keys_new, values_new, key_cache, value_cache, block_lists, block_counts, visible_blocks
):
    n = lax.axis_size("seq")
    sections = lax.axis_size("section")
    spans, rows = queries.shape[1], queries.shape[2]
    heads, context = key_cache.shape[1], key_cache.shape[2]
    kv_dev = max(1, heads // GROUP)
    span_len = rows * n
    items = 2 * kv_dev + heads
    slots = block_lists.shape[4]
    smem = pl.BlockSpec(memory_space=pltpu.MemorySpace.SMEM)
    vmem = pl.BlockSpec(memory_space=pltpu.MemorySpace.VMEM)
    anywhere = pl.BlockSpec(memory_space=pl.ANY)
    relayed = max(1, spans * heads - DIRECT)
    tiles = span_len // ROW_TILE
    cols = -(-heads * spans * (span_len // BLK) // LANES) * LANES
    dma = pltpu.SemaphoreType.DMA
    return pl.pallas_call(
        functools.partial(fused, n, sections),
        out_shape=pltpu.VMEM(queries.shape, queries.dtype),
        in_specs=[smem, vmem, vmem] + [anywhere] * 5,
        out_specs=vmem,
        scratch_shapes=[
            pltpu.VMEM((spans, heads, span_len, DH), jnp.bfloat16),
            pltpu.VMEM((spans, kv_dev, span_len, DH), jnp.bfloat16),
            pltpu.VMEM((spans, kv_dev, span_len, DH), jnp.bfloat16),
            pltpu.VMEM((heads, context, DH), jnp.bfloat16),
            pltpu.VMEM((heads, context, DH), jnp.bfloat16),
            pltpu.VMEM((context, cols), jnp.bfloat16),
            pltpu.VMEM((spans, heads, span_len, DH), jnp.bfloat16),
            pltpu.VMEM((tiles, ROW_TILE, context + span_len), jnp.float32),
            pltpu.VMEM((tiles, ROW_TILE, LANES), jnp.float32),
            dma((spans, items)),
            dma((spans, items)),
            dma((2, heads)),
            dma((1,)),
            dma((1,)),
            pltpu.VMEM((relayed, span_len, DH), jnp.bfloat16),
            dma((relayed,)),
            dma((1,)),
            pltpu.SemaphoreType.REGULAR,
        ],
        compiler_params=pltpu.CompilerParams(
            collective_id=0, has_side_effects=True, vmem_limit_bytes=60 << 20
        ),
    )(
        visible_blocks,
        block_lists.reshape(-1, slots),
        block_counts,
        queries,
        keys_new,
        values_new,
        key_cache,
        value_cache,
    )


def solution(mesh):
    return jax.shard_map(
        on_device,
        mesh=mesh,
        in_specs=(
            P("section", None, "seq", None),
            P("section", None, "seq", None),
            P("section", None, "seq", None),
            P("section", "seq", None, None),
            P("section", "seq", None, None),
            P("section", "seq", None, None, None),
            P("section", "seq", None, None),
            P(),
        ),
        out_specs=P("section", None, "seq", None),
        check_vma=False,
    )
```

```python
import functools
import math

import jax
import jax.numpy as jnp
from jax import lax
from jax.experimental import pallas as pl
from jax.experimental.pallas import tpu as pltpu
from jax.sharding import PartitionSpec as P

DH = 128
BLK = 64
GROUP = 4
LANES = 128
ROW_TILE = 256
CHUNK = 512
FAR = -1e30
DIRECT = 4
LAG = 3


def mesh_copy(src, dst, send_sem, recv_sem, section, seq):
    return pltpu.make_async_remote_copy(
        src_ref=src,
        dst_ref=dst,
        send_sem=send_sem,
        recv_sem=recv_sem,
        device_id=(section, seq),
        device_id_type=pl.DeviceIdType.MESH,
    )


def scores_of(query, keys):
    return lax.dot_general(
        query, keys, (((1,), (1,)), ((), ())), preferred_element_type=jnp.float32
    )


def whole_max(best, scores):
    for i in range(0, scores.shape[1], LANES):
        part = scores[:, i : i + LANES]
        best = part if best is None else jnp.maximum(best, part)
    return best


def fused(
    n,
    sections,
    visible_in,
    lists_in,
    counts_in,
    queries,
    keys_new,
    values_new,
    key_cache,
    value_cache,
    out,
    qbuf,
    kbuf,
    vbuf,
    ckeys,
    cvalues,
    reach,
    att,
    score_buf,
    top_buf,
    in_send,
    in_recv,
    cache_sem,
    out_send,
    out_recv,
    stage,
    stage_recv,
    pass_send,
    visible,
    lists,
    counts,
    table_sem,
    gate,
):
    spans, heads, span_len = qbuf.shape[0], qbuf.shape[1], qbuf.shape[2]
    context = ckeys.shape[1]
    kv_dev = kbuf.shape[1]
    rows = queries.shape[2]
    slots = lists.shape[1]
    query_blocks = span_len // BLK
    items = 2 * kv_dev + heads
    tiles = span_len // ROW_TILE
    columns = reach.shape[1]
    weight_scale = math.log2(math.e) / math.sqrt(DH)
    section = lax.axis_index("section")
    me = lax.axis_index("seq")
    above = lax.rem(section + 1, sections)
    below = lax.rem(section + sections - 1, sections)

    def key_copy(head):
        return pltpu.make_async_copy(key_cache.at[0, head], ckeys.at[head], cache_sem.at[0, head])

    def value_copy(head):
        return pltpu.make_async_copy(
            value_cache.at[0, head], cvalues.at[head], cache_sem.at[1, head]
        )

    def source(span, item, seq):
        if isinstance(item, int) and item < 2 * kv_dev:
            array = keys_new if item < kv_dev else values_new
            column = lax.div(seq * heads, GROUP) * DH + (item % kv_dev) * DH
        else:
            array = queries
            column = (seq * heads + item - 2 * kv_dev) * DH
        return array.at[0, span, :, pl.ds(pl.multiple_of(column, DH), DH)]

    def landing(span, item, seq):
        where = pl.ds(pl.multiple_of(seq * rows, rows), rows)
        if isinstance(item, int) and item < kv_dev:
            return kbuf.at[span, item, where, :]
        if isinstance(item, int) and item < 2 * kv_dev:
            return vbuf.at[span, item - kv_dev, where, :]
        return qbuf.at[span, item - 2 * kv_dev, where, :]

    def own_copy(span, item):
        return pltpu.make_async_copy(
            source(span, item, me), landing(span, item, me), in_recv.at[span, item]
        )

    def in_copy(span, item, k):
        seq_to = lax.rem(me + k, n)
        return mesh_copy(
            source(span, item, seq_to),
            landing(span, item, me),
            in_send.at[span, item],
            in_recv.at[span, item],
            section,
            seq_to,
        )

    def received(span, item, count):
        where = pl.ds(0, count * rows)
        if isinstance(item, int) and item < kv_dev:
            return kbuf.at[span, item, where, :]
        if isinstance(item, int) and item < 2 * kv_dev:
            return vbuf.at[span, item - kv_dev, where, :]
        return qbuf.at[span, item - 2 * kv_dev, where, :]

    def await_in(span, item):
        whole = received(span, item, n)
        pltpu.make_async_copy(whole, whole, in_recv.at[span, item]).wait()

    def await_sent(span, item):
        most = received(span, item, n - 1)
        pltpu.make_async_copy(most, most, in_send.at[span, item]).wait()

    order = [2 * kv_dev] + list(range(2 * kv_dev)) + list(range(2 * kv_dev + 1, items))

    barrier = pltpu.get_barrier_semaphore()

    def greet(k, carry):
        pl.semaphore_signal(
            barrier,
            inc=1,
            device_id=(section, lax.rem(me + k, n)),
            device_id_type=pl.DeviceIdType.MESH,
        )
        return carry

    lax.fori_loop(1, n, greet, 0)
    for there in (above, below):
        pl.semaphore_signal(
            barrier, inc=1, device_id=(there, me), device_id_type=pl.DeviceIdType.MESH
        )
    pl.semaphore_wait(barrier, n + 1)

    tables = [
        pltpu.make_async_copy(there, here, table_sem.at[i])
        for i, (there, here) in enumerate(
            [(visible_in, visible), (lists_in, lists), (counts_in, counts)]
        )
    ]

    def send_items(span, some):
        for item in some:

            def send_in(k, carry):
                in_copy(span, item, k).start()
                return carry

            lax.fori_loop(1, n, send_in, 0)
        for item in some:
            own_copy(span, item).start()

    urgent = 1 + 2 * kv_dev
    send_items(0, order[:urgent])
    for table in tables:
        table.start()

    pl.semaphore_signal(gate, inc=1, device_id=(below, me), device_id_type=pl.DeviceIdType.MESH)

    for head in range(heads):
        key_copy(head).start()
        value_copy(head).start()

    units = spans * heads
    relayed = max(1, units - DIRECT)

    def out_piece(buffer, span, head, seq_from, seq_to):
        column = pl.multiple_of((seq_from * heads + head) * DH, DH)
        where = pl.ds(pl.multiple_of(seq_to * rows, rows), rows)
        return buffer.at[where, :], out.at[0, span, :, pl.ds(column, DH)]

    def out_copy(span, head, k):
        seq_to = lax.rem(me + k, n)
        source_ref, target_ref = out_piece(att.at[span, head], span, head, me, seq_to)
        return mesh_copy(source_ref, target_ref, out_send.at[0], out_recv.at[0], above, seq_to)

    def up_copy(span, head, tile):
        where = pl.ds(tile * ROW_TILE, ROW_TILE)
        unit = span * heads + head
        return mesh_copy(
            att.at[span, head, where, :],
            stage.at[unit, where, :],
            out_send.at[0],
            stage_recv.at[unit],
            above,
            me,
        )

    def pass_on(unit):
        span, head = unit // heads, unit % heads
        whole = stage.at[unit]
        pltpu.make_async_copy(whole, whole, stage_recv.at[unit]).wait()
        source_ref, target_ref = out_piece(whole, span, head, me, me)
        pltpu.make_async_copy(source_ref, target_ref, out_recv.at[0]).start()

        def one(k, carry):
            seq_to = lax.rem(me + k, n)
            source_ref, target_ref = out_piece(whole, span, head, me, seq_to)
            mesh_copy(
                source_ref, target_ref, pass_send.at[0], out_recv.at[0], section, seq_to
            ).start()
            return carry

        lax.fori_loop(1, n, one, 0)

    def pass_after(unit):
        return max(1, unit + LAG, units // 2 - 1 + (unit > 0))

    def build_reach():
        lane = lax.broadcasted_iota(jnp.int32, (1, columns), 1)
        group = lax.div(lane, query_blocks)
        count = jnp.zeros((1, columns), jnp.float32)
        place = lax.rem(lax.broadcasted_iota(jnp.int32, (query_blocks, columns), 1), query_blocks)
        spread = jnp.where(
            place == lax.broadcasted_iota(jnp.int32, (query_blocks, columns), 0), 1.0, 0.0
        ).astype(jnp.bfloat16)
        span_at = lax.broadcasted_iota(jnp.int32, (spans, columns), 0)
        group_at = lax.div(lax.broadcasted_iota(jnp.int32, (spans, columns), 1), query_blocks)
        for head in range(heads):
            wide = jnp.dot(
                counts[0, head].astype(jnp.float32).astype(jnp.bfloat16),
                spread,
                preferred_element_type=jnp.float32,
            )
            wide = jnp.where(group_at == head * spans + span_at, wide, 0.0)
            count = count + jnp.sum(wide, axis=0, keepdims=True)
        seen = jnp.zeros((1, columns), jnp.int32)
        for span in range(spans):
            seen = jnp.where(lax.rem(group, spans) == span, visible[span], seen)
        seen = seen.astype(jnp.float32)
        eye = jnp.where(
            lax.broadcasted_iota(jnp.int32, (slots, slots), 0)
            == lax.broadcasted_iota(jnp.int32, (slots, slots), 1),
            1.0,
            0.0,
        ).astype(jnp.bfloat16)
        listed = lists[...].astype(jnp.float32)
        if columns > listed.shape[0]:
            listed = jnp.concatenate(
                [listed, jnp.zeros((columns - listed.shape[0], slots), jnp.float32)], axis=0
            )
        listed = scores_of(eye, listed.astype(jnp.bfloat16))
        slot = lax.broadcasted_iota(jnp.int32, (slots, columns), 0).astype(jnp.float32)
        listed = jnp.where((slot < count) & (listed < seen), listed, -1.0)
        blocks = context // BLK
        block = lax.broadcasted_iota(jnp.int32, (blocks, columns), 0).astype(jnp.float32)
        bias = jnp.full((blocks, columns), FAR, jnp.float32)
        for i in range(slots):
            bias = jnp.where(listed[i : i + 1, :] == block, 0.0, bias)
        for j in range(blocks):
            reach[j * BLK : (j + 1) * BLK, :] = jnp.broadcast_to(
                bias[j : j + 1, :], (BLK, columns)
            ).astype(jnp.bfloat16)

    for table in tables:
        table.wait()
    build_reach()
    pl.semaphore_wait(gate, 1)

    row_at = lax.broadcasted_iota(jnp.int32, (ROW_TILE, ROW_TILE), 0)
    key_at = lax.broadcasted_iota(jnp.int32, (ROW_TILE, ROW_TILE), 1)
    mark_row = lax.div(lax.broadcasted_iota(jnp.int32, (ROW_TILE, columns), 0), BLK)
    mark_lane = lax.broadcasted_iota(jnp.int32, (ROW_TILE, columns), 1)

    def score_steps(span, head, kv, tile):
        slot = tile
        at = slice(tile * ROW_TILE, (tile + 1) * ROW_TILE)
        best = [None]
        first = (head * spans + span) * query_blocks + tile * (ROW_TILE // BLK)

        def keep(scores, start):
            score_buf[slot, :, start : start + scores.shape[1]] = scores
            best[0] = whole_max(best[0], scores)

        def cache(start):
            mark = jnp.where(mark_lane == mark_row + first, 1.0, 0.0).astype(jnp.bfloat16)
            query = jnp.concatenate([qbuf[span, head, at, :], mark], axis=1)
            keys = jnp.concatenate(
                [ckeys[head, start : start + CHUNK, :], reach[start : start + CHUNK, :]], axis=1
            )
            keep(scores_of(query, keys), start)

        def own(piece):
            keys = kbuf[span, kv, piece * ROW_TILE : (piece + 1) * ROW_TILE, :]
            scores = scores_of(qbuf[span, head, at, :], keys)
            if piece == tile:
                scores = jnp.where(row_at >= key_at, scores, FAR)
            keep(scores, context + piece * ROW_TILE)

        def finish():
            top = jnp.max(best[0], axis=1, keepdims=True)
            top_buf[slot] = jnp.broadcast_to(top, (ROW_TILE, LANES))

        return (
            [functools.partial(cache, start) for start in range(0, context, CHUNK)],
            [functools.partial(own, piece) for piece in range(tile + 1)] + [finish],
        )

    def value_steps(span, head, kv, tile):
        slot = tile
        total = [None]

        def part(start, values):
            top = top_buf[slot]
            size = values.shape[0]
            weights = []
            for i in range(start, start + size, LANES):
                scores = score_buf[slot, :, i : i + LANES]
                weights.append(jnp.exp2((scores - top) * weight_scale).astype(jnp.bfloat16))
            values = jnp.concatenate([values, jnp.ones((size, LANES), jnp.bfloat16)], axis=1)
            product = jnp.dot(
                jnp.concatenate(weights, axis=1), values, preferred_element_type=jnp.float32
            )
            total[0] = product if total[0] is None else total[0] + product

        def cache(start):
            part(start, cvalues[head, start : start + CHUNK, :])

        def own(piece):
            part(
                context + piece * ROW_TILE,
                vbuf[span, kv, piece * ROW_TILE : (piece + 1) * ROW_TILE, :],
            )

        def finish():
            mixed = total[0][:, :DH] / total[0][:, DH:]
            att[span, head, tile * ROW_TILE : (tile + 1) * ROW_TILE, :] = mixed.astype(
                jnp.bfloat16
            )

        return (
            [functools.partial(cache, start) for start in range(0, context, CHUNK)]
            + [functools.partial(own, piece) for piece in range(tile + 1)]
            + [finish]
        )

    def together(first, second):
        for i in range(max(len(first), len(second))):
            if i < len(first):
                first[i]()
            if i < len(second):
                second[i]()

    def first_unit():
        key_copy(0).wait()
        value_copy(0).wait()
        await_in(0, 2 * kv_dev)
        steps = [score_steps(0, 0, 0, tile) for tile in range(tiles)]
        for cached, _ in steps:
            for step in cached:
                step()
        send_items(0, order[urgent:])
        for span in range(1, spans):
            send_items(span, order)
        for item in range(2 * kv_dev):
            await_in(0, item)
        for step in steps[0][1]:
            step()
        for tile in range(tiles):
            later = steps[tile + 1][1] if tile + 1 < tiles else []
            together(later, value_steps(0, 0, 0, tile))
        for tile in range(tiles):
            up_copy(0, 0, tile).start()

    def one_unit(unit, carry):
        span, head = lax.div(unit, heads), lax.rem(unit, heads)
        kv = lax.div(head, GROUP)

        @pl.when(head == 0)
        def _():
            for item in range(2 * kv_dev):
                await_in(span, item)

        @pl.when(span == 0)
        def _():
            key_copy(head).wait()
            value_copy(head).wait()

        await_in(span, 2 * kv_dev + head)
        for steps in score_steps(span, head, kv, 0):
            for step in steps:
                step()
        for tile in range(tiles):
            later = []
            if tile + 1 < tiles:
                later = sum(score_steps(span, head, kv, tile + 1), [])
            together(later, value_steps(span, head, kv, tile))

        @pl.when(unit < relayed)
        def _():
            for tile in range(tiles):
                up_copy(span, head, tile).start()

        @pl.when(unit >= relayed)
        def _():
            def send_out(k, inner):
                out_copy(span, head, k).start()
                return inner

            lax.fori_loop(0, n, send_out, 0)

        for done in range(relayed):

            @pl.when(unit == pass_after(done))
            def _():
                pass_on(done)

        return carry

    first_unit()
    lax.fori_loop(1, units, one_unit, 0)
    for done in range(relayed):
        if pass_after(done) >= units:
            pass_on(done)

    for span in range(spans):
        for item in range(items):
            await_sent(span, item)
    pltpu.make_async_copy(att, att, out_send.at[0]).wait()
    passed = stage.at[:, pl.ds(0, (n - 1) * rows), :]
    pltpu.make_async_copy(passed, passed, pass_send.at[0]).wait()
    pltpu.make_async_copy(out, out, out_recv.at[0]).wait()


def on_device(
    queries, keys_new, values_new, key_cache, value_cache, block_lists, block_counts, visible_blocks
):
    n = lax.axis_size("seq")
    sections = lax.axis_size("section")
    spans, rows = queries.shape[1], queries.shape[2]
    heads, context = key_cache.shape[1], key_cache.shape[2]
    kv_dev = max(1, heads // GROUP)
    span_len = rows * n
    items = 2 * kv_dev + heads
    slots = block_lists.shape[4]
    vmem = pl.BlockSpec(memory_space=pltpu.MemorySpace.VMEM)
    anywhere = pl.BlockSpec(memory_space=pl.ANY)
    relayed = max(1, spans * heads - DIRECT)
    tiles = span_len // ROW_TILE
    cols = -(-heads * spans * (span_len // BLK) // LANES) * LANES
    dma = pltpu.SemaphoreType.DMA
    return pl.pallas_call(
        functools.partial(fused, n, sections),
        out_shape=pltpu.VMEM(queries.shape, queries.dtype),
        in_specs=[anywhere] * 8,
        out_specs=vmem,
        scratch_shapes=[
            pltpu.VMEM((spans, heads, span_len, DH), jnp.bfloat16),
            pltpu.VMEM((spans, kv_dev, span_len, DH), jnp.bfloat16),
            pltpu.VMEM((spans, kv_dev, span_len, DH), jnp.bfloat16),
            pltpu.VMEM((heads, context, DH), jnp.bfloat16),
            pltpu.VMEM((heads, context, DH), jnp.bfloat16),
            pltpu.VMEM((context, cols), jnp.bfloat16),
            pltpu.VMEM((spans, heads, span_len, DH), jnp.bfloat16),
            pltpu.VMEM((tiles, ROW_TILE, context + span_len), jnp.float32),
            pltpu.VMEM((tiles, ROW_TILE, LANES), jnp.float32),
            dma((spans, items)),
            dma((spans, items)),
            dma((2, heads)),
            dma((1,)),
            dma((1,)),
            pltpu.VMEM((relayed, span_len, DH), jnp.bfloat16),
            dma((relayed,)),
            dma((1,)),
            pltpu.SMEM(visible_blocks.shape, jnp.int32),
            pltpu.VMEM((heads * spans * (span_len // BLK), slots), jnp.int32),
            pltpu.VMEM(block_counts.shape, jnp.int32),
            dma((3,)),
            pltpu.SemaphoreType.REGULAR,
        ],
        compiler_params=pltpu.CompilerParams(
            collective_id=0, has_side_effects=True, vmem_limit_bytes=60 << 20
        ),
    )(
        visible_blocks,
        block_lists.reshape(-1, slots),
        block_counts,
        queries,
        keys_new,
        values_new,
        key_cache,
        value_cache,
    )


def solution(mesh):
    return jax.shard_map(
        on_device,
        mesh=mesh,
        in_specs=(
            P("section", None, "seq", None),
            P("section", None, "seq", None),
            P("section", None, "seq", None),
            P("section", "seq", None, None),
            P("section", "seq", None, None),
            P("section", "seq", None, None, None),
            P("section", "seq", None, None),
            P(),
        ),
        out_specs=P("section", None, "seq", None),
        check_vma=False,
    )
```

```python
import functools
import math

import jax
import jax.numpy as jnp
from jax import lax
from jax.experimental import pallas as pl
from jax.experimental.pallas import tpu as pltpu
from jax.sharding import PartitionSpec as P

DH = 128
BLK = 64
GROUP = 4
LANES = 128
ROW_TILE = 256
CHUNK = 512
FAR = -1e30
DIRECT = 4
LAG = 3


def mesh_copy(src, dst, send_sem, recv_sem, section, seq):
    return pltpu.make_async_remote_copy(
        src_ref=src,
        dst_ref=dst,
        send_sem=send_sem,
        recv_sem=recv_sem,
        device_id=(section, seq),
        device_id_type=pl.DeviceIdType.MESH,
    )


def scores_of(query, keys):
    return lax.dot_general(
        query, keys, (((1,), (1,)), ((), ())), preferred_element_type=jnp.float32
    )


def whole_max(best, scores):
    for i in range(0, scores.shape[1], LANES):
        part = scores[:, i : i + LANES]
        best = part if best is None else jnp.maximum(best, part)
    return best


def fused(
    n,
    sections,
    visible_in,
    lists_in,
    counts_in,
    queries,
    keys_new,
    values_new,
    key_cache,
    value_cache,
    out,
    qbuf,
    kbuf,
    vbuf,
    ckeys,
    cvalues,
    reach,
    att,
    score_buf,
    top_buf,
    in_send,
    in_recv,
    cache_sem,
    out_send,
    out_recv,
    stage,
    stage_recv,
    pass_send,
    visible,
    lists,
    counts,
    table_sem,
    gate,
):
    spans, heads, span_len = qbuf.shape[0], qbuf.shape[1], qbuf.shape[2]
    context = ckeys.shape[1]
    kv_dev = kbuf.shape[1]
    rows = queries.shape[2]
    slots = lists.shape[1]
    query_blocks = span_len // BLK
    items = 2 * kv_dev + heads
    tiles = span_len // ROW_TILE
    columns = reach.shape[1]
    weight_scale = math.log2(math.e) / math.sqrt(DH)
    section = lax.axis_index("section")
    me = lax.axis_index("seq")
    above = lax.rem(section + 1, sections)
    below = lax.rem(section + sections - 1, sections)

    def key_copy(head):
        return pltpu.make_async_copy(key_cache.at[0, head], ckeys.at[head], cache_sem.at[0, head])

    def value_copy(head):
        return pltpu.make_async_copy(
            value_cache.at[0, head], cvalues.at[head], cache_sem.at[1, head]
        )

    def source(span, item, seq):
        if isinstance(item, int) and item < 2 * kv_dev:
            array = keys_new if item < kv_dev else values_new
            column = lax.div(seq * heads, GROUP) * DH + (item % kv_dev) * DH
        else:
            array = queries
            column = (seq * heads + item - 2 * kv_dev) * DH
        return array.at[0, span, :, pl.ds(pl.multiple_of(column, DH), DH)]

    def landing(span, item, seq):
        where = pl.ds(pl.multiple_of(seq * rows, rows), rows)
        if isinstance(item, int) and item < kv_dev:
            return kbuf.at[span, item, where, :]
        if isinstance(item, int) and item < 2 * kv_dev:
            return vbuf.at[span, item - kv_dev, where, :]
        return qbuf.at[span, item - 2 * kv_dev, where, :]

    def own_copy(span, item):
        return pltpu.make_async_copy(
            source(span, item, me), landing(span, item, me), in_recv.at[span, item]
        )

    def in_copy(span, item, k):
        seq_to = lax.rem(me + k, n)
        return mesh_copy(
            source(span, item, seq_to),
            landing(span, item, me),
            in_send.at[span, item],
            in_recv.at[span, item],
            section,
            seq_to,
        )

    def received(span, item, count):
        where = pl.ds(0, count * rows)
        if isinstance(item, int) and item < kv_dev:
            return kbuf.at[span, item, where, :]
        if isinstance(item, int) and item < 2 * kv_dev:
            return vbuf.at[span, item - kv_dev, where, :]
        return qbuf.at[span, item - 2 * kv_dev, where, :]

    def await_in(span, item):
        whole = received(span, item, n)
        pltpu.make_async_copy(whole, whole, in_recv.at[span, item]).wait()

    def await_sent(span, item):
        most = received(span, item, n - 1)
        pltpu.make_async_copy(most, most, in_send.at[span, item]).wait()

    order = [2 * kv_dev] + list(range(2 * kv_dev)) + list(range(2 * kv_dev + 1, items))

    barrier = pltpu.get_barrier_semaphore()

    def greet(k, carry):
        pl.semaphore_signal(
            barrier,
            inc=1,
            device_id=(section, lax.rem(me + k, n)),
            device_id_type=pl.DeviceIdType.MESH,
        )
        return carry

    lax.fori_loop(1, n, greet, 0)
    for there in (above, below):
        pl.semaphore_signal(
            barrier, inc=1, device_id=(there, me), device_id_type=pl.DeviceIdType.MESH
        )
    pl.semaphore_wait(barrier, n + 1)

    tables = [
        pltpu.make_async_copy(there, here, table_sem.at[i])
        for i, (there, here) in enumerate(
            [(visible_in, visible), (lists_in, lists), (counts_in, counts)]
        )
    ]

    def send_items(span, some):
        for item in some:

            def send_in(k, carry):
                in_copy(span, item, k).start()
                return carry

            lax.fori_loop(1, n, send_in, 0)
        for item in some:
            own_copy(span, item).start()

    urgent = 1 + 2 * kv_dev
    send_items(0, order[:urgent])
    for table in tables:
        table.start()

    pl.semaphore_signal(gate, inc=1, device_id=(below, me), device_id_type=pl.DeviceIdType.MESH)

    for head in range(heads):
        key_copy(head).start()
        value_copy(head).start()

    units = spans * heads
    relayed = max(1, units - DIRECT)

    def out_piece(buffer, span, head, seq_from, seq_to):
        column = pl.multiple_of((seq_from * heads + head) * DH, DH)
        where = pl.ds(pl.multiple_of(seq_to * rows, rows), rows)
        return buffer.at[where, :], out.at[0, span, :, pl.ds(column, DH)]

    def out_copy(span, head, k):
        seq_to = lax.rem(me + 2 + k, n)
        source_ref, target_ref = out_piece(att.at[span, head], span, head, me, seq_to)
        return mesh_copy(source_ref, target_ref, out_send.at[0], out_recv.at[0], above, seq_to)

    def up_copy(span, head, tile):
        where = pl.ds(tile * ROW_TILE, ROW_TILE)
        unit = span * heads + head
        return mesh_copy(
            att.at[span, head, where, :],
            stage.at[unit, where, :],
            out_send.at[0],
            stage_recv.at[unit],
            above,
            me,
        )

    def pass_on(unit):
        span, head = unit // heads, unit % heads
        whole = stage.at[unit]
        pltpu.make_async_copy(whole, whole, stage_recv.at[unit]).wait()
        source_ref, target_ref = out_piece(whole, span, head, me, me)
        pltpu.make_async_copy(source_ref, target_ref, out_recv.at[0]).start()

        def one(k, carry):
            seq_to = lax.rem(me + k, n)
            source_ref, target_ref = out_piece(whole, span, head, me, seq_to)
            mesh_copy(
                source_ref, target_ref, pass_send.at[0], out_recv.at[0], section, seq_to
            ).start()
            return carry

        lax.fori_loop(1, n, one, 0)

    def pass_after(unit):
        return max(1, unit + LAG, units // 2 - 1 + (unit > 0))

    def build_reach():
        lane = lax.broadcasted_iota(jnp.int32, (1, columns), 1)
        group = lax.div(lane, query_blocks)
        count = jnp.zeros((1, columns), jnp.float32)
        place = lax.rem(lax.broadcasted_iota(jnp.int32, (query_blocks, columns), 1), query_blocks)
        spread = jnp.where(
            place == lax.broadcasted_iota(jnp.int32, (query_blocks, columns), 0), 1.0, 0.0
        ).astype(jnp.bfloat16)
        span_at = lax.broadcasted_iota(jnp.int32, (spans, columns), 0)
        group_at = lax.div(lax.broadcasted_iota(jnp.int32, (spans, columns), 1), query_blocks)
        for head in range(heads):
            wide = jnp.dot(
                counts[0, head].astype(jnp.float32).astype(jnp.bfloat16),
                spread,
                preferred_element_type=jnp.float32,
            )
            wide = jnp.where(group_at == head * spans + span_at, wide, 0.0)
            count = count + jnp.sum(wide, axis=0, keepdims=True)
        seen = jnp.zeros((1, columns), jnp.int32)
        for span in range(spans):
            seen = jnp.where(lax.rem(group, spans) == span, visible[span], seen)
        seen = seen.astype(jnp.float32)
        eye = jnp.where(
            lax.broadcasted_iota(jnp.int32, (slots, slots), 0)
            == lax.broadcasted_iota(jnp.int32, (slots, slots), 1),
            1.0,
            0.0,
        ).astype(jnp.bfloat16)
        listed = lists[...].astype(jnp.float32)
        if columns > listed.shape[0]:
            listed = jnp.concatenate(
                [listed, jnp.zeros((columns - listed.shape[0], slots), jnp.float32)], axis=0
            )
        listed = scores_of(eye, listed.astype(jnp.bfloat16))
        slot = lax.broadcasted_iota(jnp.int32, (slots, columns), 0).astype(jnp.float32)
        listed = jnp.where((slot < count) & (listed < seen), listed, -1.0)
        blocks = context // BLK
        block = lax.broadcasted_iota(jnp.int32, (blocks, columns), 0).astype(jnp.float32)
        bias = jnp.full((blocks, columns), FAR, jnp.float32)
        for i in range(slots):
            bias = jnp.where(listed[i : i + 1, :] == block, 0.0, bias)
        for j in range(blocks):
            reach[j * BLK : (j + 1) * BLK, :] = jnp.broadcast_to(
                bias[j : j + 1, :], (BLK, columns)
            ).astype(jnp.bfloat16)

    for table in tables:
        table.wait()
    build_reach()
    pl.semaphore_wait(gate, 1)

    row_at = lax.broadcasted_iota(jnp.int32, (ROW_TILE, ROW_TILE), 0)
    key_at = lax.broadcasted_iota(jnp.int32, (ROW_TILE, ROW_TILE), 1)
    mark_row = lax.div(lax.broadcasted_iota(jnp.int32, (ROW_TILE, columns), 0), BLK)
    mark_lane = lax.broadcasted_iota(jnp.int32, (ROW_TILE, columns), 1)

    def score_steps(span, head, kv, tile):
        slot = tile
        at = slice(tile * ROW_TILE, (tile + 1) * ROW_TILE)
        best = [None]
        first = (head * spans + span) * query_blocks + tile * (ROW_TILE // BLK)

        def keep(scores, start):
            score_buf[slot, :, start : start + scores.shape[1]] = scores
            best[0] = whole_max(best[0], scores)

        def cache(start):
            mark = jnp.where(mark_lane == mark_row + first, 1.0, 0.0).astype(jnp.bfloat16)
            query = jnp.concatenate([qbuf[span, head, at, :], mark], axis=1)
            keys = jnp.concatenate(
                [ckeys[head, start : start + CHUNK, :], reach[start : start + CHUNK, :]], axis=1
            )
            keep(scores_of(query, keys), start)

        def own(piece):
            keys = kbuf[span, kv, piece * ROW_TILE : (piece + 1) * ROW_TILE, :]
            scores = scores_of(qbuf[span, head, at, :], keys)
            if piece == tile:
                scores = jnp.where(row_at >= key_at, scores, FAR)
            keep(scores, context + piece * ROW_TILE)

        def finish():
            top = jnp.max(best[0], axis=1, keepdims=True)
            top_buf[slot] = jnp.broadcast_to(top, (ROW_TILE, LANES))

        return (
            [functools.partial(cache, start) for start in range(0, context, CHUNK)],
            [functools.partial(own, piece) for piece in range(tile + 1)] + [finish],
        )

    def value_steps(span, head, kv, tile):
        slot = tile
        total = [None]

        def part(start, values):
            top = top_buf[slot]
            size = values.shape[0]
            weights = []
            for i in range(start, start + size, LANES):
                scores = score_buf[slot, :, i : i + LANES]
                weights.append(jnp.exp2((scores - top) * weight_scale).astype(jnp.bfloat16))
            values = jnp.concatenate([values, jnp.ones((size, LANES), jnp.bfloat16)], axis=1)
            product = jnp.dot(
                jnp.concatenate(weights, axis=1), values, preferred_element_type=jnp.float32
            )
            total[0] = product if total[0] is None else total[0] + product

        def cache(start):
            part(start, cvalues[head, start : start + CHUNK, :])

        def own(piece):
            part(
                context + piece * ROW_TILE,
                vbuf[span, kv, piece * ROW_TILE : (piece + 1) * ROW_TILE, :],
            )

        def finish():
            mixed = total[0][:, :DH] / total[0][:, DH:]
            att[span, head, tile * ROW_TILE : (tile + 1) * ROW_TILE, :] = mixed.astype(
                jnp.bfloat16
            )

        return (
            [functools.partial(cache, start) for start in range(0, context, CHUNK)]
            + [functools.partial(own, piece) for piece in range(tile + 1)]
            + [finish]
        )

    def together(first, second):
        for i in range(max(len(first), len(second))):
            if i < len(first):
                first[i]()
            if i < len(second):
                second[i]()

    def first_unit():
        key_copy(0).wait()
        value_copy(0).wait()
        await_in(0, 2 * kv_dev)
        steps = [score_steps(0, 0, 0, tile) for tile in range(tiles)]
        for cached, _ in steps:
            for step in cached:
                step()
        send_items(0, order[urgent:])
        for span in range(1, spans):
            send_items(span, order)
        for item in range(2 * kv_dev):
            await_in(0, item)
        for step in steps[0][1]:
            step()
        for tile in range(tiles):
            later = steps[tile + 1][1] if tile + 1 < tiles else []
            together(later, value_steps(0, 0, 0, tile))
        for tile in range(tiles):
            up_copy(0, 0, tile).start()

    def one_unit(unit, carry):
        span, head = lax.div(unit, heads), lax.rem(unit, heads)
        kv = lax.div(head, GROUP)

        @pl.when(head == 0)
        def _():
            for item in range(2 * kv_dev):
                await_in(span, item)

        @pl.when(span == 0)
        def _():
            key_copy(head).wait()
            value_copy(head).wait()

        await_in(span, 2 * kv_dev + head)
        for steps in score_steps(span, head, kv, 0):
            for step in steps:
                step()
        for tile in range(tiles):
            later = []
            if tile + 1 < tiles:
                later = sum(score_steps(span, head, kv, tile + 1), [])
            together(later, value_steps(span, head, kv, tile))

        @pl.when(unit < relayed)
        def _():
            for tile in range(tiles):
                up_copy(span, head, tile).start()

        @pl.when(unit >= relayed)
        def _():
            def send_out(k, inner):
                out_copy(span, head, k).start()
                return inner

            lax.fori_loop(0, n, send_out, 0)

        for done in range(relayed):

            @pl.when(unit == pass_after(done))
            def _():
                pass_on(done)

        return carry

    first_unit()
    lax.fori_loop(1, units, one_unit, 0)
    for done in range(relayed):
        if pass_after(done) >= units:
            pass_on(done)

    for span in range(spans):
        for item in range(items):
            await_sent(span, item)
    pltpu.make_async_copy(att, att, out_send.at[0]).wait()
    passed = stage.at[:, pl.ds(0, (n - 1) * rows), :]
    pltpu.make_async_copy(passed, passed, pass_send.at[0]).wait()
    pltpu.make_async_copy(out, out, out_recv.at[0]).wait()


def on_device(
    queries, keys_new, values_new, key_cache, value_cache, block_lists, block_counts, visible_blocks
):
    n = lax.axis_size("seq")
    sections = lax.axis_size("section")
    spans, rows = queries.shape[1], queries.shape[2]
    heads, context = key_cache.shape[1], key_cache.shape[2]
    kv_dev = max(1, heads // GROUP)
    span_len = rows * n
    items = 2 * kv_dev + heads
    slots = block_lists.shape[4]
    vmem = pl.BlockSpec(memory_space=pltpu.MemorySpace.VMEM)
    anywhere = pl.BlockSpec(memory_space=pl.ANY)
    relayed = max(1, spans * heads - DIRECT)
    tiles = span_len // ROW_TILE
    cols = -(-heads * spans * (span_len // BLK) // LANES) * LANES
    dma = pltpu.SemaphoreType.DMA
    return pl.pallas_call(
        functools.partial(fused, n, sections),
        out_shape=pltpu.VMEM(queries.shape, queries.dtype),
        in_specs=[anywhere] * 8,
        out_specs=vmem,
        scratch_shapes=[
            pltpu.VMEM((spans, heads, span_len, DH), jnp.bfloat16),
            pltpu.VMEM((spans, kv_dev, span_len, DH), jnp.bfloat16),
            pltpu.VMEM((spans, kv_dev, span_len, DH), jnp.bfloat16),
            pltpu.VMEM((heads, context, DH), jnp.bfloat16),
            pltpu.VMEM((heads, context, DH), jnp.bfloat16),
            pltpu.VMEM((context, cols), jnp.bfloat16),
            pltpu.VMEM((spans, heads, span_len, DH), jnp.bfloat16),
            pltpu.VMEM((tiles, ROW_TILE, context + span_len), jnp.float32),
            pltpu.VMEM((tiles, ROW_TILE, LANES), jnp.float32),
            dma((spans, items)),
            dma((spans, items)),
            dma((2, heads)),
            dma((1,)),
            dma((1,)),
            pltpu.VMEM((relayed, span_len, DH), jnp.bfloat16),
            dma((relayed,)),
            dma((1,)),
            pltpu.SMEM(visible_blocks.shape, jnp.int32),
            pltpu.VMEM((heads * spans * (span_len // BLK), slots), jnp.int32),
            pltpu.VMEM(block_counts.shape, jnp.int32),
            dma((3,)),
            pltpu.SemaphoreType.REGULAR,
        ],
        compiler_params=pltpu.CompilerParams(
            collective_id=0, has_side_effects=True, vmem_limit_bytes=60 << 20
        ),
    )(
        visible_blocks,
        block_lists.reshape(-1, slots),
        block_counts,
        queries,
        keys_new,
        values_new,
        key_cache,
        value_cache,
    )


def solution(mesh):
    return jax.shard_map(
        on_device,
        mesh=mesh,
        in_specs=(
            P("section", None, "seq", None),
            P("section", None, "seq", None),
            P("section", None, "seq", None),
            P("section", "seq", None, None),
            P("section", "seq", None, None),
            P("section", "seq", None, None, None),
            P("section", "seq", None, None),
            P(),
        ),
        out_specs=P("section", None, "seq", None),
        check_vma=False,
    )
```
